256 devices in a mesh: date: 32 (over z, x), rng: 8 (over y, core).
Axes of the slice: x: 4, y: 4, z: 8, core: 2. Of those that a mesh axis runs over, the one named last changes fastest.
Arguments:
- slc: bfloat16 [256, 2, 256, 4096], P('date', None, None, 'rng')
- offsets: int32 [256, 32, 2], P('date', 'rng'), may hold values from -2 to 2, as said below
- taps: float32 [256, 8], P('date'), may hold values from 0.05 to 1
- pairs: int32 [1024, 2], replicated, may hold values from 0 to 255, as said below
Outputs:
- series: float32 [2, 256, 64, 256], P(None, None, 'date', 'rng')
The draws below stay inside these ranges and needn't reach their ends.
Inputs may be any that keep to these rules, and one draw needn't show every extreme that they name: `offsets`: every value from -2 to 2 occurs. Every date is the reference of exactly 4 pairs; the secondary date is the reference plus 1 to min(16, 255), counted modulo 256.
All inputs are finite; a program needn't handle non-finite values.
Results may differ from the reference program's by a relative error of at most 0.0018.
Values may be sent and summed in bfloat16 or wider, within the bound.
No kernel may reach another device: no remote copies, remote signals or barrier semaphores. Data moves between devices by JAX's collectives and lax.ppermute only.
A program may use at most 256 MiB of HBM per device.

```python
import math
import jax
import jax.numpy as jnp
from jax import lax

ROWS = 256
TAPS = 8
MAXOFF = 2
LOOK_ROW = 4
LOOK_COL = 16
DATES = 256
PAIRS = 1024
COLS = 4096
TILES = 32


def draw_slc(key, part):
    keys = jax.random.split(jax.random.fold_in(key, 101), 5)
    base = jax.random.normal(keys[0], (2, ROWS, COLS), jnp.float32)
    phase = jax.random.uniform(keys[1], (DATES, 1, 1), jnp.float32, -math.pi, math.pi)
    noise = 0.6 * jax.random.normal(keys[2], (DATES, 2, ROWS, COLS), jnp.float32)
    amplitude = jnp.exp(jax.random.uniform(keys[3], (ROWS, 1), jnp.float32, 0.0, 1.15) + jax.random.uniform(keys[4], (1, COLS), jnp.float32, 0.0, 1.15))
    cosine = jnp.cos(phase)
    sine = jnp.sin(phase)
    real_part = (cosine * base[0] - sine * base[1] + noise[:, 0]) * amplitude
    imag_part = (sine * base[0] + cosine * base[1] + noise[:, 1]) * amplitude
    return jnp.stack([real_part, imag_part], axis=1).astype(jnp.bfloat16)


def draw_offsets(key, part):
    keys = jax.random.split(jax.random.fold_in(key, 202), 3)
    values = jax.random.randint(keys[0], (DATES, TILES, 2), -MAXOFF, MAXOFF + 1, dtype=jnp.int32)
    first = jax.random.randint(keys[1], (), 0, DATES, dtype=jnp.int32)
    column = jax.random.randint(keys[2], (), 0, TILES, dtype=jnp.int32)
    values = values.at[first, column].set(MAXOFF)
    values = values.at[(first + 1) % DATES, column].set(-MAXOFF)
    return values


def draw_pairs(key, part):
    keys = jax.random.split(jax.random.fold_in(key, 303), 2)
    first = jax.random.permutation(keys[0], jnp.arange(PAIRS, dtype=jnp.int32)) % DATES
    step = jax.random.randint(keys[1], (PAIRS,), 1, min(17, DATES), dtype=jnp.int32)
    second = (first + step) % DATES
    return jnp.stack([first, second], axis=1).astype(jnp.int32)


def shard_levels(rng, dims, cuts, smallest, high):
    gain, own = 1.0, jax.random.fold_in(rng, 6)
    for dim, blocks in cuts:
        draws = jnp.exp(jax.random.uniform(jax.random.fold_in(own, dim), (blocks,), jnp.float32, smallest / len(cuts), high / len(cuts)))
        gain = gain * jnp.repeat(draws, dims[dim] // blocks).reshape([-1 if axis == dim else 1 for axis in range(len(dims))])
    return gain


def setup_inputs(seed: int = 0) -> dict:
    seeds = jax.random.split(jax.random.key(seed), 5)
    return {
        "slc": draw_slc(jax.random.fold_in(seeds[4], 71), 0),
        "offsets": draw_offsets(jax.random.fold_in(seeds[4], 71), 0),
        "taps": jnp.clip(0.05 + 0.95 * jax.random.uniform(seeds[2], (DATES, TAPS), jnp.float32) ** shard_levels(seeds[2], (DATES, TAPS), ((0, 32),), -0.2, 0.2), 0.05, 1.0),
        "pairs": draw_pairs(jax.random.fold_in(seeds[4], 71), 0),
    }


EPS = 1e-06
REG = 0.1

def resample_date(padded, offs, kernel):
    width = MAXOFF + TAPS // 2
    rows = padded.shape[1] - 2 * MAXOFF
    cols = padded.shape[2] - 2 * width
    tile = cols // offs.shape[0]
    row_shift = jnp.repeat(offs[:, 0], tile, total_repeat_length=cols)
    col_shift = jnp.repeat(offs[:, 1], tile, total_repeat_length=cols)
    chosen = jnp.zeros((2, padded.shape[1], cols), jnp.float32)
    for shift in range(-MAXOFF, MAXOFF + 1):
        total = jnp.zeros((2, padded.shape[1], cols), jnp.float32)
        for k in range(TAPS):
            begin = width - shift + k - TAPS // 2 + 1
            total = total + kernel[k] * padded[:, :, begin:begin + cols].astype(jnp.float32)
        chosen = jnp.where(col_shift[None, None, :] == shift, total, chosen)
    result = jnp.zeros((2, rows, cols), jnp.float32)
    for shift in range(-MAXOFF, MAXOFF + 1):
        begin = MAXOFF - shift
        result = jnp.where(row_shift[None, None, :] == shift, chosen[:, begin:begin + rows, :], result)
    return result.astype(jnp.bfloat16)

def multilook(field):
    lead = field.shape[:-2]
    rows, cols = (field.shape[-2], field.shape[-1])
    shaped = field.reshape(lead + (rows // LOOK_ROW, LOOK_ROW, cols // LOOK_COL, LOOK_COL))
    return lax.optimization_barrier(jnp.sum(shaped, axis=(-3, -1)))

def coherence(stack, power, block):
    first_ids = block[:, 0]
    second_ids = block[:, 1]
    first = jnp.take(stack, first_ids, axis=0).astype(jnp.float32)
    second = jnp.take(stack, second_ids, axis=0).astype(jnp.float32)
    real_part = multilook(first[:, 0] * second[:, 0] + first[:, 1] * second[:, 1])
    imag_part = multilook(first[:, 1] * second[:, 0] - first[:, 0] * second[:, 1])
    scale = 1.0 / jnp.sqrt(jnp.take(power, first_ids, axis=0) * jnp.take(power, second_ids, axis=0) + EPS)
    return jnp.stack([real_part * scale, imag_part * scale], axis=1)

def invert(pairs, coher, dates):
    count = coher.shape[0]
    iota = jnp.arange(dates, dtype=jnp.int32)[None, :]
    design = (pairs[:, 0:1] == iota).astype(jnp.float32) - (pairs[:, 1:2] == iota).astype(jnp.float32)
    normal = jnp.dot(design.T.astype(jnp.float32), design.astype(jnp.float32), precision=lax.Precision.HIGHEST, preferred_element_type=jnp.float32)
    normal = normal + REG * jnp.eye(dates, dtype=jnp.float32)
    rhs = jnp.dot(design.T.astype(jnp.float32), coher.reshape(count, -1).astype(jnp.float32), precision=lax.Precision.HIGHEST, preferred_element_type=jnp.float32)
    factor = jnp.linalg.cholesky(normal)
    solved = jax.scipy.linalg.cho_solve((factor, True), rhs)
    shaped = solved.reshape((dates,) + coher.shape[1:])
    return jnp.transpose(shaped, (1, 0, 2, 3))

def reference(slc, offsets, taps, pairs):
    width = MAXOFF + TAPS // 2

    def one_date(item):
        field, offs, kernel = item
        padded = jnp.pad(field, ((0, 0), (MAXOFF, MAXOFF), (width, width)))
        return resample_date(padded, offs, kernel)
    resampled = lax.map(one_date, (slc, offsets, taps))

    def date_power(field):
        values = field.astype(jnp.float32)
        return multilook(values[0] * values[0] + values[1] * values[1])
    power = lax.map(date_power, resampled)
    blocks = pairs.reshape(PAIRS // 8, 8, 2)
    coher = lax.map(lambda block: coherence(resampled, power, block), blocks)
    coher = coher.reshape((PAIRS,) + coher.shape[2:])
    return invert(pairs, coher, DATES)
```

```python
import functools

import jax
import jax.numpy as jnp
from jax import lax
from jax.experimental import pallas as pl
from jax.experimental.pallas import tpu as pltpu
from jax.sharding import Mesh
from jax.sharding import PartitionSpec as P

TAPS = 8
EPS = 1e-06
REG = 0.1
DATES = 256
PAIRS = 1024
UNIT = 8
WINDOW = 48
REFS = 32
SLOTS = 4
NEWTON = 9
CHUNKS = ((1, 2), (0,), (3,))

F32 = jnp.float32
BF16 = jnp.bfloat16


def iota(shape, dim):
    return lax.broadcasted_iota(jnp.int32, shape, dim)


def dot(a, b, precision=None):
    return jnp.dot(a, b, precision=precision, preferred_element_type=F32)


def split(v):
    high = v.astype(BF16)
    return high, (v - high.astype(F32)).astype(BF16)


def resample_kernel(tiles, needed, halo_in, pack, off_ref, taps_ref, x_ref, *refs):
    refs = list(refs)
    data = {t: refs.pop(0) for t in needed}
    halo = {t: refs.pop(0) for t in halo_in}
    outs = [refs.pop(0) for _ in range(4)]
    packs = [refs.pop(0) for _ in range(2)] if pack else None
    perm = refs.pop(0)
    d = pl.program_id(0)

    @pl.when(d == 0)
    def _():
        o = iota((256, 256), 0)
        region = (x_ref[0] + (o >> 6)) & 3
        row = 32 * (o & 7) + 8 * region + 4 * ((o >> 3) & 1) + ((o >> 4) & 3)
        gap = row - iota((256, 256), 1)
        for s in range(5):
            perm[s] = jnp.where(gap == s - 2, 1.0, 0.0).astype(BF16)
        if pack:
            for ref in packs:
                ref[...] = jnp.zeros_like(ref)

    if pack:
        j, l = iota((128, 128), 0), iota((128, 128), 1)
        left = jnp.where((j < 8) & (l == 8 * d + j), 1.0, 0.0).astype(BF16)
        right = jnp.where((j >= 120) & (l == 16 + 8 * d + j - 120), 1.0, 0.0).astype(BF16)
        for c in range(2):
            packs[0][c] += dot(data[0][0, c], left).astype(BF16)
            packs[1][c] += dot(data[3][0, c], right).astype(BF16)

    j = iota((256, 128), 0)
    lane = iota((256, 128), 1)
    m = j - 128
    for n, t in enumerate(tiles):
        row_shift = off_ref[d, 2 * t]
        col_shift = off_ref[d, 2 * t + 1]
        if t == 0:
            own = m - 16 - 8 * d
            side = jnp.where(m < 16, 128 + m, jnp.where((own >= 0) & (own < 8), own - 8, -4096))
        elif t == 3:
            own = m - 8 * d
            side = jnp.where(m >= 112, m - 128, jnp.where((own >= 0) & (own < 8), 128 + own, -4096))
        else:
            side = jnp.where(m < 64, 128 + m, m - 128)
        k = jnp.where(j < 128, j, side) - lane + col_shift + 3
        band = jnp.zeros((256, 128), F32)
        for tap in range(TAPS):
            band = jnp.where(k == tap, taps_ref[d, tap], band)
        high, low = split(band)
        weights = jnp.concatenate([high, low], axis=1)
        at = iota((256, 128), 1)
        parts = []
        for c in range(2):
            cur = data[t][0, c]
            if t == 0:
                mixed = jnp.where(at < 16, data[1][0, c], halo[0][c])
            elif t == 3:
                mixed = jnp.where(at < 112, halo[3][c], data[2][0, c])
            else:
                mixed = jnp.where(at < 64, data[t + 1][0, c], data[t - 1][0, c])
            wide = dot(jnp.concatenate([cur, mixed], axis=1), weights)
            parts.append((wide[:, :128] + wide[:, 128:]).astype(BF16))
        moved = dot(perm[row_shift + 2], jnp.concatenate(parts, axis=1)).astype(BF16)
        for g in range(4):
            for c in range(2):
                outs[g][n, 0, c] = moved[64 * g : 64 * g + 64, 128 * c : 128 * c + 128]


def resample(tiles, slc, halos, offs, taps, x, pack):
    needed = sorted({s for t in tiles for s in (t - 1, t, t + 1) if 0 <= s < 4})
    halo_in = [t for t in tiles if t in (0, 3)]
    count = len(tiles)
    whole = pl.BlockSpec((2, 256, 128), lambda d, *_: (0, 0, 0))
    in_specs = [
        pl.BlockSpec((1, 2, 256, 128), functools.partial(lambda t, d, *_: (d, 0, 0, t), t))
        for t in needed
    ] + [whole] * len(halo_in)
    out_specs = [pl.BlockSpec((count, 1, 2, 64, 128), lambda d, *_: (0, d, 0, 0, 0))] * 4
    out_shape = [jax.ShapeDtypeStruct((count, UNIT, 2, 64, 128), BF16)] * 4
    if pack:
        out_specs += [whole] * 2
        out_shape += [jax.ShapeDtypeStruct((2, 256, 128), BF16)] * 2
    return pl.pallas_call(
        functools.partial(resample_kernel, tiles, needed, halo_in, pack),
        out_shape=out_shape,
        grid_spec=pltpu.PrefetchScalarGridSpec(
            num_scalar_prefetch=3,
            grid=(UNIT,),
            in_specs=in_specs,
            out_specs=out_specs,
            scratch_shapes=[pltpu.VMEM((5, 256, 256), BF16)],
        ),
        name="resample" + "".join(map(str, tiles)),
    )(offs, taps, x, *([slc] * len(needed)), *[halos[t] for t in halo_in])


def table_kernel(first_ref, pairs_ref, out_ref):
    a, b = pairs_ref[0:1, :], pairs_ref[1:2, :]
    date = (iota((REFS, PAIRS), 0) + first_ref[0]) & (DATES - 1)
    key = jnp.where(a == date, iota((REFS, PAIRS), 1) * DATES + b, 1 << 20)
    lane = iota((REFS, 128), 1)
    w = iota((REFS, 128), 0)
    out = jnp.zeros((REFS, 128), jnp.int32)
    for s in range(SLOTS):
        low = jnp.min(key, axis=1, keepdims=True)
        key = jnp.where(key == low, 1 << 20, key)
        away = ((low & (DATES - 1)) - w - first_ref[0]) & (DATES - 1)
        out = jnp.where(lane == s, w + away, out)
    out_ref[...] = out


def table(first, pairs_t):
    return pl.pallas_call(
        table_kernel,
        out_shape=jax.ShapeDtypeStruct((REFS, 128), jnp.int32),
        grid_spec=pltpu.PrefetchScalarGridSpec(
            num_scalar_prefetch=1,
            grid=(1,),
            in_specs=[pl.BlockSpec((2, PAIRS), lambda i, *_: (0, 0))],
            out_specs=pl.BlockSpec((REFS, 128), lambda i, *_: (0, 0)),
        ),
        name="table",
    )(first, pairs_t)


def inverse_kernel(pairs_ref, out_ref):
    high = lax.Precision.HIGHEST
    date = iota((DATES, PAIRS), 0)
    one = jnp.where(pairs_ref[0:1, :] == date, 1.0, 0.0)
    design = (one - jnp.where(pairs_ref[1:2, :] == date, 1.0, 0.0)).astype(BF16)
    normal = lax.dot_general(
        design, design, (((1,), (1,)), ((), ())), preferred_element_type=F32
    )
    eye = jnp.where(iota((DATES, DATES), 0) == iota((DATES, DATES), 1), 1.0, 0.0)
    top = 2.0 * jnp.max(normal, keepdims=True) + REG
    normal = normal + REG * eye
    rho = (top - REG) / (top + REG)
    start = 2.0 / (top + REG)
    square = rho * rho
    beta = 2.0 / (2.0 - square)
    rho = square / (2.0 - square)
    x = (beta * start) * (2.0 * eye - start * normal)

    def step(_, carry):
        x, rho = carry
        square = rho * rho
        beta = 2.0 / (2.0 - square)
        y = 2.0 * eye - dot(normal, x, high)
        return beta * dot(x, y, high), square / (2.0 - square)

    out_ref[...] = lax.fori_loop(0, NEWTON, step, (x, rho))[0]


def inverse(pairs_t):
    return pl.pallas_call(
        inverse_kernel,
        out_shape=jax.ShapeDtypeStruct((DATES, DATES), F32),
        name="inverse",
    )(pairs_t)


def fold(v):
    return v[0:16] + v[16:32] + v[32:48] + v[48:64]


def coherence_kernel(tiles, first, last, tab_ref, *refs):
    refs = list(refs)
    units = [refs.pop(0) for _ in range(6)]
    before = None if first else refs.pop(0)
    out_ref = refs.pop(0)
    win, sums_h, sums_l, pow_h, pow_l, raw, power, rhs, sem = refs
    copies = [
        [
            pltpu.make_async_copy(
                units[u].at[n], win.at[n, pl.ds(UNIT * u, UNIT)], sem.at[n, u]
            )
            for u in range(6)
        ]
        for n in range(len(tiles))
    ]
    for group in copies:
        for copy in group:
            copy.start()
    if first:
        rhs[...] = jnp.zeros_like(rhs)
    else:
        rhs[...] = before[...]
    k, l = iota((512, 128), 0), iota((512, 128), 1)
    kp, lp = iota((256, 128), 0), iota((256, 128), 1)
    for n, t in enumerate(tiles):
        for copy in copies[n]:
            copy.wait()

        def power_step(i, _):
            row = pl.multiple_of(i * 16, 16)
            tops = []
            for e in range(2):
                v = win[n, 2 * i + e].astype(F32)
                tops.append(fold(v[0] * v[0] + v[1] * v[1]))
            for h in range(2):
                v = jnp.concatenate([s[8 * h : 8 * h + 8] for s in tops], axis=0)
                hi, lo = split(v)
                pow_h[pl.ds(row, 16), 128 * h : 128 * h + 128] = hi
                pow_l[pl.ds(row, 16), 128 * h : 128 * h + 128] = lo
            return 0

        lax.fori_loop(0, WINDOW // 2, power_step, 0)

        def pair_step(w, _):
            a = win[n, w].astype(F32)
            for half in range(2):
                got = []
                for s in (2 * half, 2 * half + 1):
                    b = win[n, tab_ref[w, s]].astype(F32)
                    re = fold(a[0] * b[0] + a[1] * b[1])
                    im = fold(a[1] * b[0] - a[0] * b[1])
                    got.append((re[0:8], re[8:16], im[0:8], im[8:16]))
                row = pl.multiple_of(w * 32 + 16 * half, 16)
                for g in range(4):
                    hi, lo = split(jnp.concatenate([got[0][g], got[1][g]], axis=0))
                    sums_h[pl.ds(row, 16), 128 * g : 128 * g + 128] = hi
                    sums_l[pl.ds(row, 16), 128 * g : 128 * g + 128] = lo
            return 0

        lax.fori_loop(0, REFS, pair_step, 0)
        sel = jnp.where(l == 32 * (k >> 7) + 8 * t + ((k & 127) >> 4), 1.0, 0.0).astype(BF16)
        selp = jnp.where(
            (lp & 63) == 32 * (kp >> 7) + 8 * t + ((kp & 127) >> 4), 1.0, 0.0
        ).astype(BF16)
        r = dot(sums_h[...], sel) + dot(sums_l[...], sel)
        p = dot(pow_h[...], selp) + dot(pow_l[...], selp)
        raw[...] = r if n == 0 else raw[...] + r
        power[...] = p if n == 0 else power[...] + p

    def scale_step(w, _):
        row = pl.multiple_of(w * 8, 8)
        pa = power[pl.ds(row, 8), :]
        total = jnp.zeros((8, 128), F32)
        parts = []
        for s in range(SLOTS):
            at = pl.multiple_of(tab_ref[w, s] * 8, 8)
            pb = power[pl.ds(at, 8), :]
            v = raw[pl.ds(pl.multiple_of(w * 32 + 8 * s, 8), 8), :]
            v = v * (1.0 / jnp.sqrt(pa * pb + EPS))
            total = total + v
            parts.append((at, v))
        rhs[pl.ds(row, 8), :] += total
        for at, v in parts:
            rhs[pl.ds(at, 8), :] -= v
        return 0

    lax.fori_loop(0, REFS, scale_step, 0, unroll=2)
    if last:
        for z in range(8):
            out_ref[z] = rhs[pl.ds(z, WINDOW, stride=8), :]
    else:
        out_ref[...] = rhs[...]


def coherence(tiles, tab, units, before, last):
    count = len(tiles)
    first = before is None
    shape = (8, WINDOW, 128) if last else (WINDOW * 8, 128)
    extra = [] if first else [before]
    return pl.pallas_call(
        functools.partial(coherence_kernel, tiles, first, last),
        out_shape=jax.ShapeDtypeStruct(shape, F32),
        in_specs=[pl.BlockSpec(memory_space=pltpu.SMEM)]
        + [pl.BlockSpec(memory_space=pl.ANY)] * 6
        + [pl.BlockSpec(memory_space=pltpu.VMEM)] * len(extra),
        out_specs=pl.BlockSpec(memory_space=pltpu.VMEM),
        scratch_shapes=[
            pltpu.VMEM((count, WINDOW, 2, 64, 128), BF16),
            pltpu.VMEM((PAIRS, 512), BF16),
            pltpu.VMEM((PAIRS, 512), BF16),
            pltpu.VMEM((WINDOW * 8, 256), BF16),
            pltpu.VMEM((WINDOW * 8, 256), BF16),
            pltpu.VMEM((PAIRS, 128), F32),
            pltpu.VMEM((WINDOW * 8, 128), F32),
            pltpu.VMEM((WINDOW * 8, 128), F32),
            pltpu.SemaphoreType.DMA((count, 6)),
        ],
        name="coherence" + "".join(map(str, tiles)),
    )(tab, *units, *extra)


def solve_kernel(x_ref, inv_ref, got_ref, out_ref, rhs):
    rhs[...] = jnp.zeros_like(rhs)
    for z in range(8):
        for u in range(6):
            row = pl.multiple_of(((4 * z + x_ref[0] + 30 + u) & 31) * 8, 8)
            rhs[pl.ds(row, 8), :] += got_ref[z, 8 * u : 8 * u + 8, :]
    out_ref[...] = dot(inv_ref[...], rhs[...], lax.Precision.HIGHEST)


def solve(x, inv, got):
    return pl.pallas_call(
        solve_kernel,
        out_shape=jax.ShapeDtypeStruct((DATES, 128), F32),
        in_specs=[pl.BlockSpec(memory_space=pltpu.SMEM)]
        + [pl.BlockSpec(memory_space=pltpu.VMEM)] * 2,
        out_specs=pl.BlockSpec(memory_space=pltpu.VMEM),
        scratch_shapes=[pltpu.VMEM((DATES, 128), F32)],
        name="solve",
    )(x, inv, got)


def date_shift(v, step):
    return lax.ppermute(v, ("z", "x"), [(i, (i + step) % 32) for i in range(32)])


def per_device(slc, offsets, taps, pairs):
    x = lax.axis_index("x").astype(jnp.int32)
    unit = lax.axis_index("z").astype(jnp.int32) * 4 + x
    xs = x.reshape(1)
    offs = offsets.reshape(UNIT, 8)
    pairs_t = pairs.T
    halos = {}
    units = []
    for n, tiles in enumerate(CHUNKS):
        got = resample(tiles, slc, halos, offs, taps, xs, n == 0)
        if n == 0:
            size = lax.axis_size("rng")
            halos[3] = lax.ppermute(got[4], "rng", [(i + 1, i) for i in range(size - 1)])
            halos[0] = lax.ppermute(got[5], "rng", [(i, i + 1) for i in range(size - 1)])
        own, ahead, across, behind = got[:4]
        minus1 = date_shift(ahead, 1)
        plus1 = date_shift(behind, -1)
        plus2 = date_shift(across, -2)
        minus2 = date_shift(plus2, 4)
        plus3 = date_shift(minus1, -4)
        units.append((minus2, minus1, own, plus1, plus2, plus3))
    tab = table((unit * 8 - 16).reshape(1), pairs_t)
    inv = inverse(pairs_t)
    rhs = None
    for n, tiles in enumerate(CHUNKS):
        rhs = coherence(tiles, tab, units[n], rhs, n == len(CHUNKS) - 1)
    got = lax.all_to_all(rhs, "z", split_axis=0, concat_axis=0, tiled=True)
    series = solve(xs, inv, got)
    return jnp.transpose(series.reshape(DATES, 2, 2, 32), (1, 0, 2, 3))


def solution(mesh):
    fine = Mesh(mesh.devices.reshape(8, 4, 8), ("z", "x", "rng"))
    date = ("z", "x")
    return jax.shard_map(
        per_device,
        mesh=fine,
        in_specs=(P(date, None, None, "rng"), P(date, "rng", None), P(date, None), P()),
        out_specs=P(None, None, date, "rng"),
        check_vma=False,
    )
```

```python
import functools

import jax
import jax.numpy as jnp
from jax import lax
from jax.experimental import pallas as pl
from jax.experimental.pallas import tpu as pltpu
from jax.sharding import Mesh
from jax.sharding import PartitionSpec as P

TAPS = 8
EPS = 1e-06
REG = 0.1
DATES = 256
PAIRS = 1024
UNIT = 8
WINDOW = 48
REFS = 32
SLOTS = 4
NEWTON = 9
STEP = 4
UNROLL = 2
CHUNKS = ((1, 2), (0,), (3,))

F32 = jnp.float32
BF16 = jnp.bfloat16


def iota(shape, dim):
    return lax.broadcasted_iota(jnp.int32, shape, dim)


def dot(a, b, precision=None):
    return jnp.dot(a, b, precision=precision, preferred_element_type=F32)


def split(v):
    high = v.astype(BF16)
    return high, (v - high.astype(F32)).astype(BF16)


def resample_kernel(tiles, needed, halo_in, pack, off_ref, taps_ref, x_ref, *refs):
    refs = list(refs)
    data = {t: refs.pop(0) for t in needed}
    halo = {t: refs.pop(0) for t in halo_in}
    outs = [refs.pop(0) for _ in range(4)]
    packs = [refs.pop(0) for _ in range(2)] if pack else None
    perm = refs.pop(0)
    i = pl.program_id(0)

    @pl.when(i == 0)
    def _():
        o = iota((256, 256), 0)
        region = (x_ref[0] + (o >> 6)) & 3
        row = 32 * (o & 7) + 8 * region + 4 * ((o >> 3) & 1) + ((o >> 4) & 3)
        gap = row - iota((256, 256), 1)
        for s in range(5):
            perm[s] = jnp.where(gap == s - 2, 1.0, 0.0).astype(BF16)
        if pack:
            for ref in packs:
                ref[...] = jnp.zeros_like(ref)

    j, l = iota((128, 128), 0), iota((128, 128), 1)
    near = jnp.abs(j - l) < 64
    lane = iota((8, 128), 1)
    at = iota((256, 128), 1)
    for e in range(STEP):
        d = i * STEP + e
        if pack:
            left = jnp.where((j < 8) & (l == 8 * d + j), 1.0, 0.0).astype(BF16)
            right = jnp.where((j >= 120) & (l == 16 + 8 * d + j - 120), 1.0, 0.0).astype(BF16)
            for c in range(2):
                packs[0][c] += dot(data[0][e, c], left).astype(BF16)
                packs[1][c] += dot(data[3][e, c], right).astype(BF16)
        for n, t in enumerate(tiles):
            row_shift = off_ref[d, t, 0]
            k = (off_ref[d, t, 1] + 3 - lane) & 127
            base = jnp.zeros((8, 128), F32)
            for tap in range(TAPS):
                base = jnp.where(k == tap, taps_ref[d, tap], base)
            ring = pltpu.roll(jnp.concatenate([base] * 16, axis=0), 0, 1, stride=1, stride_axis=0)
            high = ring.astype(BF16).astype(F32)
            rows = []
            for part in (high, ring - high):
                own = jnp.where(near, part, 0.0)
                far = part - own
                if t == 0:
                    edge = jnp.concatenate([far[120:128]] * 16, axis=0)
                    far = jnp.where(j < 16, far, jnp.where((j >> 3) == 2 + d, edge, 0.0))
                elif t == 3:
                    edge = jnp.concatenate([far[0:8]] * 16, axis=0)
                    far = jnp.where(j >= 112, far, jnp.where((j >> 3) == d, edge, 0.0))
                rows.append(jnp.concatenate([own.astype(BF16), far.astype(BF16)], axis=0))
            weights = jnp.concatenate(rows, axis=1)
            parts = []
            for c in range(2):
                cur = data[t][e, c]
                if t == 0:
                    mixed = jnp.where(at < 16, data[1][e, c], halo[0][c])
                elif t == 3:
                    mixed = jnp.where(at < 112, halo[3][c], data[2][e, c])
                else:
                    mixed = jnp.where(at < 64, data[t + 1][e, c], data[t - 1][e, c])
                wide = dot(jnp.concatenate([cur, mixed], axis=1), weights)
                parts.append((wide[:, :128] + wide[:, 128:]).astype(BF16))
            moved = dot(perm[row_shift + 2], jnp.concatenate(parts, axis=1)).astype(BF16)
            for g in range(4):
                for c in range(2):
                    outs[g][n, e, c] = moved[64 * g : 64 * g + 64, 128 * c : 128 * c + 128]


def resample(tiles, slc, halos, offs, taps, x, pack):
    needed = sorted({s for t in tiles for s in (t - 1, t, t + 1) if 0 <= s < 4})
    halo_in = [t for t in tiles if t in (0, 3)]
    count = len(tiles)
    whole = pl.BlockSpec((2, 256, 128), lambda d, *_: (0, 0, 0))
    in_specs = [
        pl.BlockSpec((STEP, 2, 256, 128), functools.partial(lambda t, d, *_: (d, 0, 0, t), t))
        for t in needed
    ] + [whole] * len(halo_in)
    out_specs = [pl.BlockSpec((count, STEP, 2, 64, 128), lambda d, *_: (0, d, 0, 0, 0))] * 4
    out_shape = [jax.ShapeDtypeStruct((count, UNIT, 2, 64, 128), BF16)] * 4
    if pack:
        out_specs += [whole] * 2
        out_shape += [jax.ShapeDtypeStruct((2, 256, 128), BF16)] * 2
    return pl.pallas_call(
        functools.partial(resample_kernel, tiles, needed, halo_in, pack),
        out_shape=out_shape,
        grid_spec=pltpu.PrefetchScalarGridSpec(
            num_scalar_prefetch=3,
            grid=(UNIT // STEP,),
            in_specs=in_specs,
            out_specs=out_specs,
            scratch_shapes=[pltpu.VMEM((5, 256, 256), BF16)],
        ),
        name="resample" + "".join(map(str, tiles)),
    )(offs, taps, x, *([slc] * len(needed)), *[halos[t] for t in halo_in])


def table_kernel(first_ref, pairs_ref, out_ref):
    a, b = pairs_ref[0:1, :], pairs_ref[1:2, :]
    date = (iota((REFS, PAIRS), 0) + first_ref[0]) & (DATES - 1)
    key = jnp.where(a == date, iota((REFS, PAIRS), 1) * DATES + b, 1 << 20)
    lane = iota((REFS, 128), 1)
    w = iota((REFS, 128), 0)
    out = jnp.zeros((REFS, 128), jnp.int32)
    for s in range(SLOTS):
        low = jnp.min(key, axis=1, keepdims=True)
        key = jnp.where(key == low, 1 << 20, key)
        away = ((low & (DATES - 1)) - w - first_ref[0]) & (DATES - 1)
        out = jnp.where(lane == s, w + away, out)
    out_ref[...] = out


def table(first, pairs_t):
    return pl.pallas_call(
        table_kernel,
        out_shape=jax.ShapeDtypeStruct((REFS, 128), jnp.int32),
        grid_spec=pltpu.PrefetchScalarGridSpec(
            num_scalar_prefetch=1,
            grid=(1,),
            in_specs=[pl.BlockSpec((2, PAIRS), lambda i, *_: (0, 0))],
            out_specs=pl.BlockSpec((REFS, 128), lambda i, *_: (0, 0)),
        ),
        name="table",
    )(first, pairs_t)


def inverse_kernel(pairs_ref, out_ref):
    date = iota((DATES, PAIRS), 0)
    one = jnp.where(pairs_ref[0:1, :] == date, 1.0, 0.0)
    design = (one - jnp.where(pairs_ref[1:2, :] == date, 1.0, 0.0)).astype(BF16)
    graph = lax.dot_general(
        design, design, (((1,), (1,)), ((), ())), preferred_element_type=F32
    )
    eye = jnp.where(iota((DATES, DATES), 0) == iota((DATES, DATES), 1), 1.0, 0.0)
    top = 2.0 * jnp.max(graph, keepdims=True) + REG
    rho = (top - REG) / (top + REG)
    start = 2.0 / (top + REG)
    square = rho * rho
    beta = 2.0 / (2.0 - square)
    rho = square / (2.0 - square)
    x = (beta * start) * (2.0 * eye - start * (graph + REG * eye))
    whole = graph.astype(BF16)

    def step(_, carry):
        x, rho = carry
        square = rho * rho
        beta = 2.0 / (2.0 - square)
        high, mid = split(x)
        low = (x - high.astype(F32) - mid.astype(F32)).astype(BF16)
        gap = eye - REG * x - (dot(whole, low) + dot(whole, mid) + dot(whole, high))
        gap_h, gap_l = split(gap)
        more = dot(high, gap_l) + dot(mid, gap_h) + dot(high, gap_h)
        return beta * (x + more), square / (2.0 - square)

    out_ref[...] = lax.fori_loop(0, NEWTON, step, (x, rho))[0]


def inverse(pairs_t):
    return pl.pallas_call(
        inverse_kernel,
        out_shape=jax.ShapeDtypeStruct((DATES, DATES), F32),
        name="inverse",
    )(pairs_t)


def fold(v):
    return v[0:16] + v[16:32] + v[32:48] + v[48:64]


def coherence_kernel(tiles, first, last, tab_ref, *refs):
    refs = list(refs)
    units = [refs.pop(0) for _ in range(6)]
    raw0, power0 = (None, None) if first else (refs.pop(0), refs.pop(0))
    if last:
        out_ref, win, sums_h, sums_l, pow_h, pow_l, sem, raw, power, rhs = refs
    else:
        raw, power, win, sums_h, sums_l, pow_h, pow_l, sem = refs
    copies = [
        [
            pltpu.make_async_copy(
                units[u].at[n], win.at[n, pl.ds(UNIT * u, UNIT)], sem.at[n, u]
            )
            for u in range(6)
        ]
        for n in range(len(tiles))
    ]
    for group in copies:
        for copy in group:
            copy.start()
    k, l = iota((512, 128), 0), iota((512, 128), 1)
    kp, lp = iota((256, 128), 0), iota((256, 128), 1)
    for n, t in enumerate(tiles):
        for copy in copies[n]:
            copy.wait()

        def power_step(i, _):
            row = pl.multiple_of(i * 16, 16)
            tops = []
            for e in range(2):
                v = win[n, 2 * i + e].astype(F32)
                tops.append(fold(v[0] * v[0] + v[1] * v[1]))
            for h in range(2):
                v = jnp.concatenate([s[8 * h : 8 * h + 8] for s in tops], axis=0)
                hi, lo = split(v)
                pow_h[pl.ds(row, 16), 128 * h : 128 * h + 128] = hi
                pow_l[pl.ds(row, 16), 128 * h : 128 * h + 128] = lo
            return 0

        lax.fori_loop(0, WINDOW // 2, power_step, 0, unroll=UNROLL)

        def pair_step(w, _):
            a = win[n, w].astype(F32)
            for half in range(2):
                got = []
                for s in (2 * half, 2 * half + 1):
                    b = win[n, tab_ref[w, s]].astype(F32)
                    re = fold(a[0] * b[0] + a[1] * b[1])
                    im = fold(a[1] * b[0] - a[0] * b[1])
                    got.append((re[0:8], re[8:16], im[0:8], im[8:16]))
                row = pl.multiple_of(w * 32 + 16 * half, 16)
                for g in range(4):
                    hi, lo = split(jnp.concatenate([got[0][g], got[1][g]], axis=0))
                    sums_h[pl.ds(row, 16), 128 * g : 128 * g + 128] = hi
                    sums_l[pl.ds(row, 16), 128 * g : 128 * g + 128] = lo
            return 0

        lax.fori_loop(0, REFS, pair_step, 0, unroll=UNROLL)
        sel = jnp.where(l == 32 * (k >> 7) + 8 * t + ((k & 127) >> 4), 1.0, 0.0).astype(BF16)
        selp = jnp.where(
            (lp & 63) == 32 * (kp >> 7) + 8 * t + ((kp & 127) >> 4), 1.0, 0.0
        ).astype(BF16)
        r = dot(sums_h[...], sel) + dot(sums_l[...], sel)
        p = dot(pow_h[...], selp) + dot(pow_l[...], selp)
        if n == 0 and first:
            raw[...] = r
            power[...] = p
        elif n == 0:
            raw[...] = raw0[...] + r
            power[...] = power0[...] + p
        else:
            raw[...] += r
            power[...] += p
    if not last:
        return
    rhs[...] = jnp.zeros_like(rhs)

    def scale_step(w, _):
        row = pl.multiple_of(w * 8, 8)
        pa = power[pl.ds(row, 8), :]
        total = jnp.zeros((8, 128), F32)
        for s in range(SLOTS):
            pb = power[pl.ds(pl.multiple_of(tab_ref[w, s] * 8, 8), 8), :]
            at = pl.multiple_of(w * 32 + 8 * s, 8)
            v = raw[pl.ds(at, 8), :] * (1.0 / jnp.sqrt(pa * pb + EPS))
            total = total + v
            raw[pl.ds(at, 8), :] = v
        rhs[SLOTS, pl.ds(row, 8), :] = total
        return 0

    lax.fori_loop(0, REFS, scale_step, 0, unroll=4)

    def scatter_step(w, _):
        for s in range(SLOTS):
            at = pl.multiple_of(tab_ref[w, s] * 8, 8)
            rhs[s, pl.ds(at, 8), :] -= raw[pl.ds(pl.multiple_of(w * 32 + 8 * s, 8), 8), :]
        return 0

    lax.fori_loop(0, REFS, scatter_step, 0, unroll=4)
    rhs[SLOTS] = (rhs[0] + rhs[1]) + (rhs[2] + rhs[3]) + rhs[SLOTS]
    for z in range(8):
        out_ref[z] = rhs[SLOTS, pl.ds(z, WINDOW, stride=8), :]


def coherence(tiles, tab, units, before, last):
    count = len(tiles)
    vmem = pl.BlockSpec(memory_space=pltpu.VMEM)
    sums = [jax.ShapeDtypeStruct((SLOTS * REFS * 8, 128), F32), jax.ShapeDtypeStruct((WINDOW * 8, 128), F32)]
    scratch = [
        pltpu.VMEM((count, WINDOW, 2, 64, 128), BF16),
        pltpu.VMEM((SLOTS * REFS * 8, 512), BF16),
        pltpu.VMEM((SLOTS * REFS * 8, 512), BF16),
        pltpu.VMEM((WINDOW * 8, 256), BF16),
        pltpu.VMEM((WINDOW * 8, 256), BF16),
        pltpu.SemaphoreType.DMA((count, 6)),
    ]
    if last:
        sums = jax.ShapeDtypeStruct((8, WINDOW, 128), F32)
        scratch += [
            pltpu.VMEM((SLOTS * REFS * 8, 128), F32),
            pltpu.VMEM((WINDOW * 8, 128), F32),
            pltpu.VMEM((SLOTS + 1, WINDOW * 8, 128), F32),
        ]
    return pl.pallas_call(
        functools.partial(coherence_kernel, tiles, not before, last),
        out_shape=sums,
        in_specs=[pl.BlockSpec(memory_space=pltpu.SMEM)]
        + [pl.BlockSpec(memory_space=pl.ANY)] * 6
        + [vmem] * len(before),
        out_specs=vmem if last else [vmem] * 2,
        scratch_shapes=scratch,
        name="coherence" + "".join(map(str, tiles)),
    )(tab, *units, *before)


def solve_kernel(x_ref, inv_ref, got_ref, out_ref, rhs):
    for z in range(8):
        early = got_ref[z, 0:16, :] + got_ref[(z + 7) % 8, 32:48, :]
        for copy in (0, DATES):
            rhs[copy + 32 * z : copy + 32 * z + 16, :] = early
            rhs[copy + 32 * z + 16 : copy + 32 * z + 32, :] = got_ref[z, 16:32, :]
    at = pl.multiple_of((DATES + 16 - 8 * x_ref[0]) & (DATES - 1), 8)
    out_ref[...] = lax.dot_general(
        rhs[pl.ds(at, DATES), :],
        inv_ref[...],
        (((0,), (0,)), ((), ())),
        precision=lax.Precision.HIGHEST,
        preferred_element_type=F32,
    )


def solve(x, inv, got):
    return pl.pallas_call(
        solve_kernel,
        out_shape=jax.ShapeDtypeStruct((128, DATES), F32),
        in_specs=[pl.BlockSpec(memory_space=pltpu.SMEM)]
        + [pl.BlockSpec(memory_space=pltpu.VMEM)] * 2,
        out_specs=pl.BlockSpec(memory_space=pltpu.VMEM),
        scratch_shapes=[pltpu.VMEM((2 * DATES, 128), F32)],
        name="solve",
    )(x, inv, got)


def date_shift(v, step):
    return lax.ppermute(v, ("z", "x"), [(i, (i + step) % 32) for i in range(32)])


def per_device(slc, offsets, taps, pairs):
    x = lax.axis_index("x").astype(jnp.int32)
    unit = lax.axis_index("z").astype(jnp.int32) * 4 + x
    xs = x.reshape(1)
    pairs_t = pairs.T
    halos = {}
    units = []
    for n, tiles in enumerate(CHUNKS):
        got = resample(tiles, slc, halos, offsets, taps, xs, n == 0)
        if n == 0:
            size = lax.axis_size("rng")
            halos[3] = lax.ppermute(got[4], "rng", [(i + 1, i) for i in range(size - 1)])
            halos[0] = lax.ppermute(got[5], "rng", [(i, i + 1) for i in range(size - 1)])
        own, ahead, across, behind = got[:4]
        minus1 = date_shift(ahead, 1)
        plus1 = date_shift(behind, -1)
        plus2 = date_shift(across, -2)
        minus2 = date_shift(plus2, 4)
        plus3 = date_shift(minus1, -4)
        units.append((minus2, minus1, own, plus1, plus2, plus3))
    tab = table((unit * 8 - 16).reshape(1), pairs_t)
    inv = inverse(pairs_t)
    rhs = ()
    for n, tiles in enumerate(CHUNKS):
        rhs = coherence(tiles, tab, units[n], rhs, n == len(CHUNKS) - 1)
    got = lax.all_to_all(rhs, "z", split_axis=0, concat_axis=0, tiled=True)
    series = solve(xs, inv, got)
    return jnp.transpose(series.reshape(2, 2, 32, DATES), (0, 3, 1, 2))


def solution(mesh):
    fine = Mesh(mesh.devices.reshape(8, 4, 8), ("z", "x", "rng"))
    date = ("z", "x")
    return jax.shard_map(
        per_device,
        mesh=fine,
        in_specs=(P(date, None, None, "rng"), P(date, "rng", None), P(date, None), P()),
        out_specs=P(None, None, date, "rng"),
        check_vma=False,
    )
```

```python
import functools

import jax
import jax.numpy as jnp
from jax import lax
from jax.experimental import pallas as pl
from jax.experimental.pallas import tpu as pltpu
from jax.sharding import Mesh
from jax.sharding import PartitionSpec as P


TAPS = 8
EPS = 1e-06
REG = 0.1
DATES = 256
PAIRS = 1024
UNIT = 8
WINDOW = 48
REFS = 32
INNER = (8, 24)
SLOTS = 4
NEWTON = 9
UNROLL = 4
STEP = 4
CHUNKS = ((1, 2), (0, 3))

F32 = jnp.float32
BF16 = jnp.bfloat16


def iota(shape, dim):
    return lax.broadcasted_iota(jnp.int32, shape, dim)


def dot(a, b, precision=None):
    return jnp.dot(a, b, precision=precision, preferred_element_type=F32)


def split(v):
    high = v.astype(BF16)
    return high, (v - high.astype(F32)).astype(BF16)


def resample_kernel(tiles, needed, halo_in, pack, off_ref, taps_ref, *refs):
    refs = list(refs)
    data = {t: refs.pop(0) for t in needed}
    halo = {t: refs.pop(0) for t in halo_in}
    out = refs.pop(0)
    packs = [refs.pop(0) for _ in range(2)] if pack else None
    perm = refs.pop(0)
    i = pl.program_id(0)

    @pl.when(i == 0)
    def _():
        o = iota((256, 256), 0)
        row = 32 * (o & 7) + 8 * (o >> 6) + 4 * ((o >> 3) & 1) + ((o >> 4) & 3)
        gap = row - iota((256, 256), 1)
        for s in range(5):
            perm[s] = jnp.where(gap == s - 2, 1.0, 0.0).astype(BF16)
        if pack:
            for ref in packs:
                ref[...] = jnp.zeros_like(ref)

    j, l = iota((128, 128), 0), iota((128, 128), 1)
    near = jnp.abs(j - l) < 64
    lane = iota((8, 128), 1)
    at = iota((256, 128), 1)
    if pack:
        j4, l4 = iota((128 * STEP, 128), 0), iota((128 * STEP, 128), 1)
        slot, j4 = 8 * (i * STEP + (j4 >> 7)), j4 & 127
        left = jnp.where((j4 < 8) & (l4 == slot + j4), 1.0, 0.0).astype(BF16)
        right = jnp.where((j4 >= 120) & (l4 == slot + j4 - 104), 1.0, 0.0).astype(BF16)
        for c in range(2):
            for ref, src, sel in ((packs[0], data[0], left), (packs[1], data[3], right)):
                side = jnp.concatenate([src[e, c] for e in range(STEP)], axis=1)
                ref[c] += dot(side, sel).astype(BF16)
    for e in range(STEP):
        d = i * STEP + e
        for n, t in enumerate(tiles):
            row_shift = off_ref[t, 0, d]
            k = (off_ref[t, 1, d] + 3 - lane) & 127
            base = jnp.zeros((8, 128), F32)
            for tap in range(TAPS):
                base = jnp.where(k == tap, taps_ref[d, tap], base)
            ring = pltpu.roll(jnp.concatenate([base] * 16, axis=0), 0, 1, stride=1, stride_axis=0)
            high = ring.astype(BF16).astype(F32)
            rows = []
            for part in (high, ring - high):
                own = jnp.where(near, part, 0.0)
                far = part - own
                if t == 0:
                    edge = jnp.concatenate([far[120:128]] * 16, axis=0)
                    far = jnp.where(j < 16, far, jnp.where((j >> 3) == 2 + d, edge, 0.0))
                elif t == 3:
                    edge = jnp.concatenate([far[0:8]] * 16, axis=0)
                    far = jnp.where(j >= 112, far, jnp.where((j >> 3) == d, edge, 0.0))
                rows.append(jnp.concatenate([own.astype(BF16), far.astype(BF16)], axis=0))
            weights = jnp.concatenate(rows, axis=1)
            parts = []
            for c in range(2):
                cur = data[t][e, c]
                if t == 0:
                    mixed = jnp.where(at < 16, data[1][e, c], halo[0][c])
                elif t == 3:
                    mixed = jnp.where(at < 112, halo[3][c], data[2][e, c])
                else:
                    mixed = jnp.where(at < 64, data[t + 1][e, c], data[t - 1][e, c])
                lhs = jnp.concatenate([cur, mixed], axis=1)
                wide = dot(lhs, weights)
                parts.append((wide[:, :128] + wide[:, 128:]).astype(BF16))
            both = jnp.concatenate(parts, axis=1)
            moved = dot(perm[row_shift + 2], both).astype(BF16)
            for g in range(4):
                for c in range(2):
                    out[g, n, e, c] = moved[64 * g : 64 * g + 64, 128 * c : 128 * c + 128]


def resample(tiles, slc, halos, offs, taps, pack):
    needed = {s for t in tiles for s in (t - 1, t, t + 1) if 0 <= s < 4}
    needed = sorted(needed | {0, 3} if pack else needed)
    halo_in = [t for t in tiles if t in (0, 3)]
    count = len(tiles)
    whole = pl.BlockSpec((2, 256, 128), lambda d, *_: (0, 0, 0))
    in_specs = [
        pl.BlockSpec((STEP, 2, 256, 128), functools.partial(lambda t, d, *_: (d, 0, 0, t), t))
        for t in needed
    ] + [whole] * len(halo_in)
    out_specs = [pl.BlockSpec((4, count, STEP, 2, 64, 128), lambda d, *_: (0, 0, d, 0, 0, 0))]
    out_shape = [jax.ShapeDtypeStruct((4, count, UNIT, 2, 64, 128), BF16)]
    if pack:
        out_specs += [whole] * 2
        out_shape += [jax.ShapeDtypeStruct((2, 256, 128), BF16)] * 2
    return pl.pallas_call(
        functools.partial(resample_kernel, tiles, needed, halo_in, pack),
        out_shape=out_shape,
        grid_spec=pltpu.PrefetchScalarGridSpec(
            num_scalar_prefetch=2,
            grid=(UNIT // STEP,),
            in_specs=in_specs,
            out_specs=out_specs,
            scratch_shapes=[pltpu.VMEM((5, 256, 256), BF16)],
        ),
    )(offs, taps, *([slc] * len(needed)), *[halos[t] for t in halo_in])


def table_kernel(first_ref, pairs_ref, out_ref):
    a, b = pairs_ref[0:1, :], pairs_ref[1:2, :]
    date = (iota((REFS, PAIRS), 0) + first_ref[0]) & (DATES - 1)
    key = jnp.where(a == date, iota((REFS, PAIRS), 1) * DATES + b, 1 << 20)
    lane = iota((REFS, 128), 1)
    w = iota((REFS, 128), 0)
    out = jnp.zeros((REFS, 128), jnp.int32)
    for s in range(SLOTS):
        low = jnp.min(key, axis=1, keepdims=True)
        key = jnp.where(key == low, 1 << 20, key)
        away = ((low & (DATES - 1)) - w - first_ref[0]) & (DATES - 1)
        out = jnp.where(lane == s, w + away, out)
    out_ref[...] = out


def table(first, pairs_t):
    return pl.pallas_call(
        table_kernel,
        out_shape=jax.ShapeDtypeStruct((REFS, 128), jnp.int32),
        grid_spec=pltpu.PrefetchScalarGridSpec(
            num_scalar_prefetch=1,
            grid=(1,),
            in_specs=[pl.BlockSpec((2, PAIRS), lambda i, *_: (0, 0))],
            out_specs=pl.BlockSpec((REFS, 128), lambda i, *_: (0, 0)),
        ),
        name="table",
    )(first, pairs_t)


def inverse_kernel(pairs_ref, out_ref):
    date = iota((DATES, PAIRS), 0)
    one = jnp.where(pairs_ref[0:1, :] == date, 1.0, 0.0)
    design = (one - jnp.where(pairs_ref[1:2, :] == date, 1.0, 0.0)).astype(BF16)
    graph = lax.dot_general(
        design, design, (((1,), (1,)), ((), ())), preferred_element_type=F32
    )
    eye = jnp.where(iota((DATES, DATES), 0) == iota((DATES, DATES), 1), 1.0, 0.0)
    top = 2.0 * jnp.max(graph, keepdims=True) + REG
    rho = (top - REG) / (top + REG)
    start = 2.0 / (top + REG)
    square = rho * rho
    beta = 2.0 / (2.0 - square)
    rho = square / (2.0 - square)
    x = (beta * start) * (2.0 * eye - start * (graph + REG * eye))
    whole = graph.astype(BF16)

    def step(_, carry):
        x, rho = carry
        square = rho * rho
        beta = 2.0 / (2.0 - square)
        high, mid = split(x)
        low = (x - high.astype(F32) - mid.astype(F32)).astype(BF16)
        gap = eye - REG * x - (dot(whole, low) + dot(whole, mid) + dot(whole, high))
        gap_h, gap_l = split(gap)
        more = dot(high, gap_l) + dot(mid, gap_h) + dot(high, gap_h)
        return beta * (x + more), square / (2.0 - square)

    out_ref[...] = lax.fori_loop(0, NEWTON, step, (x, rho))[0]


def inverse(pairs_t):
    return pl.pallas_call(
        inverse_kernel,
        out_shape=jax.ShapeDtypeStruct((DATES, DATES), F32),
        name="inverse",
    )(pairs_t)


HALF = 16
RAW = HALF * SLOTS * 8


def fold(v):
    return v[0:16] + v[16:32] + v[32:48] + v[48:64]


def copies_of(sources, win, sem, count):
    return [
        [
            pltpu.make_async_copy(src.at[n], win.at[n, pl.ds(UNIT * u, UNIT)], sem.at[n, u])
            for u, src in sources
        ]
        for n in range(count)
    ]


def look_sums(tiles, copies, tab_ref, place, dates, win, sums, squares, raw, power, before):
    for group in copies:
        for copy in group:
            copy.start()
    k, l = iota((512, 128), 0), iota((512, 128), 1)
    kp, lp = iota((256, 128), 0), iota((256, 128), 1)
    for n, t in enumerate(tiles):
        sel = jnp.where(l == 32 * (k >> 7) + 8 * t + ((k & 127) >> 4), 1.0, 0.0).astype(BF16)
        selp = jnp.where(
            (lp & 63) == 32 * (kp >> 7) + 8 * t + ((kp & 127) >> 4), 1.0, 0.0
        ).astype(BF16)
        for copy in copies[n]:
            copy.wait()
        row = 0
        for start, stop in dates:

            def power_step(i, _):
                tops = []
                for e in range(4):
                    v = win[n, start + 4 * i + e].astype(F32)
                    tops.append(fold(v[0] * v[0] + v[1] * v[1]))
                at = pl.ds(pl.multiple_of(row + i * 32, 32), 32)
                for h in range(2):
                    v = jnp.concatenate([v[8 * h : 8 * h + 8] for v in tops], axis=0)
                    for m, half in enumerate(split(v)):
                        squares[m, at, 128 * h : 128 * h + 128] = half
                return 0

            lax.fori_loop(0, (stop - start) // 4, power_step, 0, unroll=2)
            row += 8 * (stop - start)
        total = dot(squares[0], selp) + dot(squares[1], selp)
        if n > 0:
            total = total + power[...]
        elif before:
            total = total + before[1][...]
        power[...] = total

        def pair_step(i, _):
            w = place(i)
            a = win[n, w].astype(F32)
            for half in range(2):
                got = []
                for s in (2 * half, 2 * half + 1):
                    b = win[n, tab_ref[w, s]].astype(F32)
                    re = fold(a[0] * b[0] + a[1] * b[1])
                    im = fold(a[1] * b[0] - a[0] * b[1])
                    got.append((re[0:8], re[8:16], im[0:8], im[8:16]))
                at = pl.ds(pl.multiple_of(i * 32 + 16 * half, 16), 16)
                for g in range(4):
                    v = jnp.concatenate([got[0][g], got[1][g]], axis=0)
                    for m, part in enumerate(split(v)):
                        sums[m, at, 128 * g : 128 * g + 128] = part
            return 0

        lax.fori_loop(0, HALF, pair_step, 0, unroll=UNROLL)
        looks = dot(sums[0], sel) + dot(sums[1], sel)
        if n > 0:
            looks = looks + raw[...]
        elif before:
            looks = looks + before[0][...]
        raw[...] = looks


def scale_and_scatter(tab_ref, place, raw, whole, rhs):
    for s in range(SLOTS):
        rhs[s] = jnp.zeros_like(rhs[s])

    def scale_step(i, _):
        w = place(i)
        pa = whole[pl.ds(pl.multiple_of(w * 8, 8), 8), :]
        total = jnp.zeros((8, 128), F32)
        for s in range(SLOTS):
            pb = whole[pl.ds(pl.multiple_of(tab_ref[w, s] * 8, 8), 8), :]
            at = pl.multiple_of(i * 32 + 8 * s, 8)
            v = raw[pl.ds(at, 8), :] * lax.rsqrt(pa * pb + EPS)
            total = total + v
            raw[pl.ds(at, 8), :] = v
        rhs[SLOTS, pl.ds(pl.multiple_of(w * 8, 8), 8), :] += total
        return 0

    lax.fori_loop(0, HALF, scale_step, 0, unroll=4)

    def scatter_step(i, _):
        for s in range(SLOTS):
            at = pl.multiple_of(tab_ref[place(i), s] * 8, 8)
            rhs[s, pl.ds(at, 8), :] -= raw[pl.ds(pl.multiple_of(i * 32 + 8 * s, 8), 8), :]
        return 0

    lax.fori_loop(0, HALF, scatter_step, 0, unroll=4)
    rhs[SLOTS] = (rhs[0] + rhs[1]) + (rhs[2] + rhs[3]) + rhs[SLOTS]


def inner_kernel(tiles, first, last, tab_ref, mine, *refs):
    refs = list(refs)
    before = () if first else (refs.pop(0), refs.pop(0))
    if last:
        rhs_out, power, win, sums, squares, sem, raw, whole, rhs = refs
    else:
        raw, power, win, sums, squares, sem = refs
    copies = copies_of([(u + 1, mine.at[u]) for u in range(4)], win, sem, len(tiles))

    def place(i):
        return i + INNER[0]

    look_sums(
        tiles, copies, tab_ref, place, ((8, 40),), win, sums, squares, raw, power, before
    )
    if last:
        whole[64:320] = power[...]
        rhs[SLOTS] = jnp.zeros_like(rhs[SLOTS])
        scale_and_scatter(tab_ref, place, raw, whole, rhs)
        rhs_out[...] = rhs[SLOTS]


def outer_kernel(tiles, first, last, tab_ref, below, mine, above, *refs):
    refs = list(refs)
    before = () if first else (refs.pop(0), refs.pop(0))
    if last:
        inner_rhs, inner_power = refs.pop(0), refs.pop(0)
        out_ref, win, sums, squares, sem, raw, power, whole, rhs = refs
    else:
        raw, power, win, sums, squares, sem = refs
    sources = [(u + 1, mine.at[u]) for u in range(4)] + [(0, below), (5, above)]
    copies = copies_of(sources, win, sem, len(tiles))

    def place(i):
        return jnp.where(i < INNER[0], i, i + INNER[1] - INNER[0])

    look_sums(
        tiles,
        copies,
        tab_ref,
        place,
        ((0, 8), (40, 48)),
        win,
        sums,
        squares,
        raw,
        power,
        before,
    )
    if last:
        whole[0:64] = power[0:64]
        whole[64:320] = inner_power[...]
        whole[320:384] = power[64:128]
        rhs[SLOTS] = inner_rhs[...]
        scale_and_scatter(tab_ref, place, raw, whole, rhs)
        for z in range(8):
            out_ref[z] = rhs[SLOTS, pl.ds(z, WINDOW, stride=8), :]


def coherence(inner, tiles, tab, units, before, extra, last):
    count = len(tiles)
    rows = 256 if inner else 128
    vmem = pl.BlockSpec(memory_space=pltpu.VMEM)
    raw = jax.ShapeDtypeStruct((RAW, 128), F32)
    power = jax.ShapeDtypeStruct((rows, 128), F32)
    scratch = [
        pltpu.VMEM((count, WINDOW, 2, 64, 128), BF16),
        pltpu.VMEM((2, RAW, 512), BF16),
        pltpu.VMEM((2, rows, 256), BF16),
        pltpu.SemaphoreType.DMA((count, 6)),
    ]
    outs = [raw, power]
    if last:
        scratch.append(pltpu.VMEM((RAW, 128), F32))
        if inner:
            outs = [jax.ShapeDtypeStruct((WINDOW * 8, 128), F32), power]
        else:
            outs = jax.ShapeDtypeStruct((8, WINDOW, 128), F32)
            scratch.append(pltpu.VMEM((rows, 128), F32))
        scratch += [
            pltpu.VMEM((WINDOW * 8, 128), F32),
            pltpu.VMEM((SLOTS + 1, WINDOW * 8, 128), F32),
        ]
    return pl.pallas_call(
        functools.partial(inner_kernel if inner else outer_kernel, tiles, not before, last),
        out_shape=outs,
        in_specs=[pl.BlockSpec(memory_space=pltpu.SMEM)]
        + [pl.BlockSpec(memory_space=pl.ANY)] * len(units)
        + [vmem] * len((*before, *extra)),
        out_specs=[vmem] * 2 if isinstance(outs, list) else vmem,
        scratch_shapes=scratch,
    )(tab, *units, *before, *extra)


def solve_kernel(inv_ref, got_ref, out_ref, rhs):
    for z in range(8):
        early = got_ref[z, 0:16, :] + got_ref[(z + 7) % 8, 32:48, :]
        rhs[32 * z : 32 * z + 16, :] = early
        rhs[32 * z + 16 : 32 * z + 32, :] = got_ref[z, 16:32, :]
        if z == 0:
            rhs[DATES : DATES + 8, :] = early[0:8]
    out_ref[...] = lax.dot_general(
        rhs[8 : DATES + 8, :],
        inv_ref[...],
        (((0,), (0,)), ((), ())),
        precision=lax.Precision.HIGHEST,
        preferred_element_type=F32,
    )


def solve(inv, got):
    return pl.pallas_call(
        solve_kernel,
        out_shape=jax.ShapeDtypeStruct((128, DATES), F32),
        in_specs=[pl.BlockSpec(memory_space=pltpu.VMEM)] * 2,
        out_specs=pl.BlockSpec(memory_space=pltpu.VMEM),
        scratch_shapes=[pltpu.VMEM((DATES + 8, 128), F32)],
        name="solve",
    )(inv, got)


def per_device(slc, offsets, taps, pairs):
    pairs_t = pairs.T
    offs = jnp.transpose(offsets, (1, 2, 0))
    halos = {}
    units = []
    up = [(z, (z + 1) % 8) for z in range(8)]
    down = [(j, i) for i, j in up]
    for n, tiles in enumerate(CHUNKS):
        got = resample(tiles, slc, halos, offs, taps, n == 0)
        if n == 0:
            size = lax.axis_size("rng")
            halos[3] = lax.ppermute(got[1], "rng", [(i + 1, i) for i in range(size - 1)])
            halos[0] = lax.ppermute(got[2], "rng", [(i, i + 1) for i in range(size - 1)])
        mine = lax.all_to_all(got[0], "x", split_axis=0, concat_axis=0, tiled=True)
        below = lax.ppermute(mine[3], "z", up)
        above = lax.ppermute(mine[0], "z", down)
        units.append((below, mine, above))
    first = lax.axis_index("z").astype(jnp.int32) * 32 - 8
    tab = table(first.reshape(1), pairs_t)
    inv = inverse(pairs_t)
    ins, outs = (), ()
    for n, tiles in enumerate(CHUNKS):
        last = n == len(CHUNKS) - 1
        ins = coherence(True, tiles, tab, units[n][1:2], ins, (), last)
        outs = coherence(False, tiles, tab, units[n], outs, ins if last else (), last)
    got = lax.all_to_all(outs, "z", split_axis=0, concat_axis=0, tiled=True)
    series = solve(inv, got)
    return jnp.transpose(series.reshape(2, 2, 32, DATES), (0, 3, 1, 2))


def solution(mesh):
    fine = Mesh(mesh.devices.reshape(8, 4, 8), ("z", "x", "rng"))
    date = ("z", "x")
    return jax.shard_map(
        per_device,
        mesh=fine,
        in_specs=(P(date, None, None, "rng"), P(date, "rng", None), P(date, None), P()),
        out_specs=P(None, None, date, "rng"),
        check_vma=False,
    )
```

```python
import functools

import jax
import jax.numpy as jnp
import numpy as np
from jax import lax
from jax.experimental import pallas as pl
from jax.experimental.pallas import tpu as pltpu
from jax.sharding import Mesh
from jax.sharding import PartitionSpec as P


TAPS = 8
EPS = 1e-06
REG = 0.1
DATES = 256
PAIRS = 1024
UNIT = 8
WINDOW = 48
REFS = 32
INNER = (8, 24)
SLOTS = 4
NEWTON = 9
UNROLL = 4
STEP = 4
CHUNKS = ((1, 2), (0, 3))

F32 = jnp.float32
BF16 = jnp.bfloat16


def iota(shape, dim):
    return lax.broadcasted_iota(jnp.int32, shape, dim)


def dot(a, b, precision=None):
    return jnp.dot(a, b, precision=precision, preferred_element_type=F32)


def split(v):
    high = v.astype(BF16)
    return high, (v - high.astype(F32)).astype(BF16)


def row_moves():
    o = np.arange(256)[:, None]
    row = 32 * (o & 7) + 8 * (o >> 6) + 4 * ((o >> 3) & 1) + ((o >> 4) & 3)
    shift = np.arange(-2, 3)[:, None, None]
    return (row - shift == np.arange(256)).astype(np.float32)


def resample_kernel(tiles, needed, halo_in, pack, off_ref, taps_ref, *refs):
    refs = list(refs)
    data = {t: refs.pop(0) for t in needed}
    halo = {t: refs.pop(0) for t in halo_in}
    perm = refs.pop(0)
    out = refs.pop(0)
    packs = [refs.pop(0) for _ in range(2)] if pack else None
    i = pl.program_id(0)
    if pack:

        @pl.when(i == 0)
        def _():
            for ref in packs:
                ref[...] = jnp.zeros_like(ref)

    j, l = iota((128, 128), 0), iota((128, 128), 1)
    near = jnp.where(jnp.abs(j - l) < 64, 1.0, 0.0).astype(BF16)
    lane = iota((8, 128), 1)
    at = iota((256, 128), 1)
    if pack:
        j4, l4 = iota((128 * STEP, 128), 0), iota((128 * STEP, 128), 1)
        slot, j4 = 8 * (i * STEP + (j4 >> 7)), j4 & 127
        left = jnp.where((j4 < 8) & (l4 == slot + j4), 1.0, 0.0).astype(BF16)
        right = jnp.where((j4 >= 120) & (l4 == slot + j4 - 104), 1.0, 0.0).astype(BF16)
        for c in range(2):
            for ref, src, sel in ((packs[0], data[0], left), (packs[1], data[3], right)):
                side = jnp.concatenate([src[e, c] for e in range(STEP)], axis=1)
                ref[c] += dot(side, sel).astype(BF16)
    for e in range(STEP):
        d = i * STEP + e
        for n, t in enumerate(tiles):
            row_shift = off_ref[t, 0, d]
            k = (off_ref[t, 1, d] + 3 - lane) & 127
            base = jnp.zeros((8, 128), F32)
            for tap in range(TAPS):
                base = jnp.where(k == tap, taps_ref[d, tap], base)
            ring = pltpu.roll(jnp.concatenate([base] * 16, axis=0), 0, 1, stride=1, stride_axis=0)
            rows = []
            for part in split(ring):
                own = part * near
                far = part - own
                if t in (0, 3):
                    far = far.astype(F32)
                    edge = jnp.concatenate([far[120:128] if t == 0 else far[0:8]] * 16, axis=0)
                    keep = j < 16 if t == 0 else j >= 112
                    slot = 2 + d if t == 0 else d
                    far = jnp.where(keep, far, jnp.where((j >> 3) == slot, edge, 0.0)).astype(BF16)
                rows.append(jnp.concatenate([own, far], axis=0))
            weights = jnp.concatenate(rows, axis=1)
            parts = []
            for c in range(2):
                cur = data[t][e, c]
                if t == 0:
                    mixed = jnp.where(at < 16, data[1][e, c], halo[0][c])
                elif t == 3:
                    mixed = jnp.where(at < 112, halo[3][c], data[2][e, c])
                else:
                    mixed = jnp.where(at < 64, data[t + 1][e, c], data[t - 1][e, c])
                lhs = jnp.concatenate([cur, mixed], axis=1)
                wide = dot(lhs, weights)
                parts.append((wide[:, :128] + wide[:, 128:]).astype(BF16))
            both = jnp.concatenate(parts, axis=1)
            moved = dot(perm[row_shift + 2], both).astype(BF16)
            for g in range(4):
                for c in range(2):
                    out[g, n, e, c] = moved[64 * g : 64 * g + 64, 128 * c : 128 * c + 128]


def resample(tiles, slc, halos, offs, taps, pack):
    needed = {s for t in tiles for s in (t - 1, t, t + 1) if 0 <= s < 4}
    needed = sorted(needed | {0, 3} if pack else needed)
    halo_in = [t for t in tiles if t in (0, 3)]
    count = len(tiles)
    whole = pl.BlockSpec((2, 256, 128), lambda d, *_: (0, 0, 0))
    in_specs = [
        pl.BlockSpec((STEP, 2, 256, 128), functools.partial(lambda t, d, *_: (d, 0, 0, t), t))
        for t in needed
    ] + [pl.BlockSpec(memory_space=pltpu.VMEM)] * len(halo_in)
    in_specs.append(pl.BlockSpec((5, 256, 256), lambda d, *_: (0, 0, 0)))
    out_specs = [pl.BlockSpec((4, count, STEP, 2, 64, 128), lambda d, *_: (0, 0, d, 0, 0, 0))]
    out_shape = [jax.ShapeDtypeStruct((4, count, UNIT, 2, 64, 128), BF16)]
    if pack:
        out_specs += [whole] * 2
        out_shape += [jax.ShapeDtypeStruct((2, 256, 128), BF16)] * 2
    return pl.pallas_call(
        functools.partial(resample_kernel, tiles, needed, halo_in, pack),
        out_shape=out_shape,
        grid_spec=pltpu.PrefetchScalarGridSpec(
            num_scalar_prefetch=2,
            grid=(UNIT // STEP,),
            in_specs=in_specs,
            out_specs=out_specs,
        ),
    )(offs, taps, *([slc] * len(needed)), *[halos[t] for t in halo_in], jnp.asarray(row_moves(), BF16))


def table_kernel(first_ref, pairs_ref, out_ref):
    a, b = pairs_ref[0:1, :], pairs_ref[1:2, :]
    date = (iota((REFS, PAIRS), 0) + first_ref[0]) & (DATES - 1)
    key = jnp.where(a == date, iota((REFS, PAIRS), 1) * DATES + b, 1 << 20)
    lane = iota((REFS, 128), 1)
    w = iota((REFS, 128), 0)
    out = jnp.zeros((REFS, 128), jnp.int32)
    for s in range(SLOTS):
        low = jnp.min(key, axis=1, keepdims=True)
        key = jnp.where(key == low, 1 << 20, key)
        away = ((low & (DATES - 1)) - w - first_ref[0]) & (DATES - 1)
        out = jnp.where(lane == s, w + away, out)
    out_ref[...] = out


def table(first, pairs_t):
    return pl.pallas_call(
        table_kernel,
        out_shape=jax.ShapeDtypeStruct((REFS, 128), jnp.int32),
        grid_spec=pltpu.PrefetchScalarGridSpec(
            num_scalar_prefetch=1,
            grid=(1,),
            in_specs=[pl.BlockSpec((2, PAIRS), lambda i, *_: (0, 0))],
            out_specs=pl.BlockSpec((REFS, 128), lambda i, *_: (0, 0)),
        ),
        name="table",
    )(first, pairs_t)


def inverse_kernel(pairs_ref, out_ref):
    date = iota((DATES, PAIRS), 0)
    one = jnp.where(pairs_ref[0:1, :] == date, 1.0, 0.0)
    design = (one - jnp.where(pairs_ref[1:2, :] == date, 1.0, 0.0)).astype(BF16)
    graph = lax.dot_general(
        design, design, (((1,), (1,)), ((), ())), preferred_element_type=F32
    )
    eye = jnp.where(iota((DATES, DATES), 0) == iota((DATES, DATES), 1), 1.0, 0.0)
    top = 2.0 * jnp.max(graph, keepdims=True) + REG
    rho = (top - REG) / (top + REG)
    start = 2.0 / (top + REG)
    square = rho * rho
    beta = 2.0 / (2.0 - square)
    rho = square / (2.0 - square)
    x = (beta * start) * (2.0 * eye - start * (graph + REG * eye))
    whole = graph.astype(BF16)

    def step(_, carry):
        x, rho = carry
        square = rho * rho
        beta = 2.0 / (2.0 - square)
        high, mid = split(x)
        low = (x - high.astype(F32) - mid.astype(F32)).astype(BF16)
        gap = eye - REG * x - (dot(whole, low) + dot(whole, mid) + dot(whole, high))
        gap_h, gap_l = split(gap)
        more = dot(high, gap_l) + dot(mid, gap_h) + dot(high, gap_h)
        return beta * (x + more), square / (2.0 - square)

    out_ref[...] = lax.fori_loop(0, NEWTON, step, (x, rho))[0]


def inverse(pairs_t):
    return pl.pallas_call(
        inverse_kernel,
        out_shape=jax.ShapeDtypeStruct((DATES, DATES), F32),
        name="inverse",
    )(pairs_t)


HALF = 16
RAW = HALF * SLOTS * 8


def fold(v):
    return v[0:16] + v[16:32] + v[32:48] + v[48:64]


def copies_of(sources, win, sem, count):
    return [
        [
            pltpu.make_async_copy(src.at[n], win.at[n, pl.ds(UNIT * u, UNIT)], sem.at[n, u])
            for u, src in sources
        ]
        for n in range(count)
    ]


def look_sums(tiles, copies, tab_ref, place, dates, win, sums, squares, raw, power, before):
    for group in copies:
        for copy in group:
            copy.start()
    k, l = iota((512, 128), 0), iota((512, 128), 1)
    kp, lp = iota((256, 128), 0), iota((256, 128), 1)
    for n, t in enumerate(tiles):
        sel = jnp.where(l == 32 * (k >> 7) + 8 * t + ((k & 127) >> 4), 1.0, 0.0).astype(BF16)
        selp = jnp.where(
            (lp & 63) == 32 * (kp >> 7) + 8 * t + ((kp & 127) >> 4), 1.0, 0.0
        ).astype(BF16)
        for copy in copies[n]:
            copy.wait()
        row = 0
        for start, stop in dates:

            def power_step(i, _):
                tops = []
                for e in range(4):
                    v = win[n, start + 4 * i + e].astype(F32)
                    tops.append(fold(v[0] * v[0] + v[1] * v[1]))
                at = pl.ds(pl.multiple_of(row + i * 32, 32), 32)
                for h in range(2):
                    v = jnp.concatenate([v[8 * h : 8 * h + 8] for v in tops], axis=0)
                    for m, half in enumerate(split(v)):
                        squares[m, at, 128 * h : 128 * h + 128] = half
                return 0

            lax.fori_loop(0, (stop - start) // 4, power_step, 0, unroll=2)
            row += 8 * (stop - start)
        total = dot(squares[0], selp) + dot(squares[1], selp)
        if n > 0:
            total = total + power[...]
        elif before:
            total = total + before[1][...]
        power[...] = total

        def pair_step(i, _):
            w = place(i)
            a = win[n, w].astype(F32)
            for half in range(2):
                got = []
                for s in (2 * half, 2 * half + 1):
                    b = win[n, tab_ref[w, s]].astype(F32)
                    re = fold(a[0] * b[0] + a[1] * b[1])
                    im = fold(a[1] * b[0] - a[0] * b[1])
                    got.append((re[0:8], re[8:16], im[0:8], im[8:16]))
                at = pl.ds(pl.multiple_of(i * 32 + 16 * half, 16), 16)
                for g in range(4):
                    v = jnp.concatenate([got[0][g], got[1][g]], axis=0)
                    sums[at, 128 * g : 128 * g + 128] = v.astype(BF16)
            return 0

        lax.fori_loop(0, HALF, pair_step, 0, unroll=UNROLL)
        looks = dot(sums[...], sel)
        if n > 0:
            looks = looks + raw[...]
        elif before:
            looks = looks + before[0][...]
        raw[...] = looks


def scale_and_scatter(tab_ref, place, raw, whole, rhs):
    for s in range(SLOTS):
        rhs[s] = jnp.zeros_like(rhs[s])

    def scale_step(i, _):
        w = place(i)
        pa = whole[pl.ds(pl.multiple_of(w * 8, 8), 8), :]
        total = jnp.zeros((8, 128), F32)
        for s in range(SLOTS):
            pb = whole[pl.ds(pl.multiple_of(tab_ref[w, s] * 8, 8), 8), :]
            at = pl.multiple_of(i * 32 + 8 * s, 8)
            v = raw[pl.ds(at, 8), :] * lax.rsqrt(pa * pb + EPS)
            total = total + v
            raw[pl.ds(at, 8), :] = v
        rhs[SLOTS, pl.ds(pl.multiple_of(w * 8, 8), 8), :] += total
        return 0

    lax.fori_loop(0, HALF, scale_step, 0, unroll=4)

    def scatter_step(i, _):
        for s in range(SLOTS):
            at = pl.multiple_of(tab_ref[place(i), s] * 8, 8)
            rhs[s, pl.ds(at, 8), :] -= raw[pl.ds(pl.multiple_of(i * 32 + 8 * s, 8), 8), :]
        return 0

    lax.fori_loop(0, HALF, scatter_step, 0, unroll=4)
    rhs[SLOTS] = (rhs[0] + rhs[1]) + (rhs[2] + rhs[3]) + rhs[SLOTS]


def inner_kernel(tiles, first, last, tab_ref, mine, *refs):
    refs = list(refs)
    before = () if first else (refs.pop(0), refs.pop(0))
    if last:
        rhs_out, power, win, sums, squares, sem, raw, whole, rhs = refs
    else:
        raw, power, win, sums, squares, sem = refs
    copies = copies_of([(u + 1, mine.at[u]) for u in range(4)], win, sem, len(tiles))

    def place(i):
        return i + INNER[0]

    look_sums(
        tiles, copies, tab_ref, place, ((8, 40),), win, sums, squares, raw, power, before
    )
    if last:
        whole[64:320] = power[...]
        rhs[SLOTS] = jnp.zeros_like(rhs[SLOTS])
        scale_and_scatter(tab_ref, place, raw, whole, rhs)
        rhs_out[...] = rhs[SLOTS]


def outer_kernel(tiles, first, last, tab_ref, below, mine, above, *refs):
    refs = list(refs)
    before = () if first else (refs.pop(0), refs.pop(0))
    if last:
        inner_rhs, inner_power = refs.pop(0), refs.pop(0)
        out_ref, win, sums, squares, sem, raw, power, whole, rhs = refs
    else:
        raw, power, win, sums, squares, sem = refs
    sources = [(u + 1, mine.at[u]) for u in range(4)] + [(0, below), (5, above)]
    copies = copies_of(sources, win, sem, len(tiles))

    def place(i):
        return jnp.where(i < INNER[0], i, i + INNER[1] - INNER[0])

    look_sums(
        tiles,
        copies,
        tab_ref,
        place,
        ((0, 8), (40, 48)),
        win,
        sums,
        squares,
        raw,
        power,
        before,
    )
    if last:
        whole[0:64] = power[0:64]
        whole[64:320] = inner_power[...]
        whole[320:384] = power[64:128]
        rhs[SLOTS] = inner_rhs[...]
        scale_and_scatter(tab_ref, place, raw, whole, rhs)
        for z in range(8):
            out_ref[z] = rhs[SLOTS, pl.ds(z, WINDOW, stride=8), :]


def coherence(inner, tiles, tab, units, before, extra, last):
    count = len(tiles)
    rows = 256 if inner else 128
    vmem = pl.BlockSpec(memory_space=pltpu.VMEM)
    raw = jax.ShapeDtypeStruct((RAW, 128), F32)
    power = jax.ShapeDtypeStruct((rows, 128), F32)
    scratch = [
        pltpu.VMEM((count, WINDOW, 2, 64, 128), BF16),
        pltpu.VMEM((RAW, 512), BF16),
        pltpu.VMEM((2, rows, 256), BF16),
        pltpu.SemaphoreType.DMA((count, 6)),
    ]
    outs = [raw, power]
    if last:
        scratch.append(pltpu.VMEM((RAW, 128), F32))
        if inner:
            outs = [jax.ShapeDtypeStruct((WINDOW * 8, 128), F32), power]
        else:
            outs = jax.ShapeDtypeStruct((8, WINDOW, 128), F32)
            scratch.append(pltpu.VMEM((rows, 128), F32))
        scratch += [
            pltpu.VMEM((WINDOW * 8, 128), F32),
            pltpu.VMEM((SLOTS + 1, WINDOW * 8, 128), F32),
        ]
    return pl.pallas_call(
        functools.partial(inner_kernel if inner else outer_kernel, tiles, not before, last),
        out_shape=outs,
        in_specs=[pl.BlockSpec(memory_space=pltpu.SMEM)]
        + [vmem if len(units) == 3 and u != 1 else pl.BlockSpec(memory_space=pl.ANY) for u in range(len(units))]
        + [vmem] * len((*before, *extra)),
        out_specs=[vmem] * 2 if isinstance(outs, list) else vmem,
        scratch_shapes=scratch,
    )(tab, *units, *before, *extra)


def solve_kernel(inv_ref, got_ref, out_ref, rhs):
    for z in range(8):
        early = got_ref[z, 0:16, :] + got_ref[(z + 7) % 8, 32:48, :]
        rhs[32 * z : 32 * z + 16, :] = early
        rhs[32 * z + 16 : 32 * z + 32, :] = got_ref[z, 16:32, :]
        if z == 0:
            rhs[DATES : DATES + 8, :] = early[0:8]
    out_ref[...] = lax.dot_general(
        rhs[8 : DATES + 8, :],
        inv_ref[...],
        (((0,), (0,)), ((), ())),
        precision=lax.Precision.HIGHEST,
        preferred_element_type=F32,
    )


def solve(inv, got):
    return pl.pallas_call(
        solve_kernel,
        out_shape=jax.ShapeDtypeStruct((128, DATES), F32),
        in_specs=[pl.BlockSpec(memory_space=pltpu.VMEM)] * 2,
        out_specs=pl.BlockSpec(memory_space=pltpu.VMEM),
        scratch_shapes=[pltpu.VMEM((DATES + 8, 128), F32)],
        name="solve",
    )(inv, got)


def near_by(v):
    return pltpu.with_memory_space_constraint(v, pltpu.VMEM)


def per_device(slc, offsets, taps, pairs):
    pairs_t = pairs.T
    offs = jnp.transpose(offsets, (1, 2, 0))
    halos = {}
    units = []
    up = [(z, (z + 1) % 8) for z in range(8)]
    down = [(j, i) for i, j in up]
    for n, tiles in enumerate(CHUNKS):
        got = resample(tiles, slc, halos, offs, taps, n == 0)
        if n == 0:
            size = lax.axis_size("rng")
            halos[3] = near_by(lax.ppermute(got[1], "rng", [(i + 1, i) for i in range(size - 1)]))
            halos[0] = near_by(lax.ppermute(got[2], "rng", [(i, i + 1) for i in range(size - 1)]))
        mine = lax.all_to_all(got[0], "x", split_axis=0, concat_axis=0, tiled=True)
        below = near_by(lax.ppermute(mine[3], "z", up))
        above = near_by(lax.ppermute(mine[0], "z", down))
        units.append((below, mine, above))
    first = lax.axis_index("z").astype(jnp.int32) * 32 - 8
    tab = table(first.reshape(1), pairs_t)
    inv = inverse(pairs_t)
    ins, outs = (), ()
    for n, tiles in enumerate(CHUNKS):
        last = n == len(CHUNKS) - 1
        ins = coherence(True, tiles, tab, units[n][1:2], ins, (), last)
        outs = coherence(False, tiles, tab, units[n], outs, ins if last else (), last)
    got = near_by(lax.all_to_all(outs, "z", split_axis=0, concat_axis=0, tiled=True))
    series = solve(inv, got)
    return jnp.transpose(series.reshape(2, 2, 32, DATES), (0, 3, 1, 2))


def solution(mesh):
    fine = Mesh(mesh.devices.reshape(8, 4, 8), ("z", "x", "rng"))
    date = ("z", "x")
    return jax.shard_map(
        per_device,
        mesh=fine,
        in_specs=(P(date, None, None, "rng"), P(date, "rng", None), P(date, None), P()),
        out_specs=P(None, None, date, "rng"),
        check_vma=False,
    )
```

```python
import functools

import jax
import jax.numpy as jnp
import numpy as np
from jax import lax
from jax.experimental import pallas as pl
from jax.experimental.pallas import tpu as pltpu
from jax.sharding import Mesh
from jax.sharding import PartitionSpec as P


TAPS = 8
EPS = 1e-06
REG = 0.1
DATES = 256
PAIRS = 1024
UNIT = 8
WINDOW = 48
REFS = 32
INNER = (8, 24)
SLOTS = 4
NEWTON = 9
UNROLL = 4
STEP = 4
CHUNKS = ((1, 2), (0, 3))

F32 = jnp.float32
BF16 = jnp.bfloat16


def iota(shape, dim):
    return lax.broadcasted_iota(jnp.int32, shape, dim)


def dot(a, b, precision=None):
    return jnp.dot(a, b, precision=precision, preferred_element_type=F32)


def split(v):
    high = v.astype(BF16)
    return high, (v - high.astype(F32)).astype(BF16)


def row_moves():
    o = np.arange(256)[:, None]
    row = 32 * (o & 7) + 8 * (o >> 6) + 4 * ((o >> 3) & 1) + ((o >> 4) & 3)
    shift = np.arange(-2, 3)[:, None, None]
    return (row - shift == np.arange(256)).astype(np.float32)


def resample_kernel(tiles, needed, halo_in, pack, off_ref, taps_ref, x_ref, *refs):
    refs = list(refs)
    data = {t: refs.pop(0) for t in needed}
    halo = {t: refs.pop(0) for t in halo_in}
    perm = refs.pop(0)
    outs = [refs.pop(0) for _ in range(4)]
    packs = [refs.pop(0) for _ in range(2)] if pack else None
    i = pl.program_id(0)
    if pack:

        @pl.when(i == 0)
        def _():
            for ref in packs:
                ref[...] = jnp.zeros_like(ref)

    j, l = iota((128, 128), 0), iota((128, 128), 1)
    near = jnp.where(jnp.abs(j - l) < 64, 1.0, 0.0).astype(BF16)
    lane = iota((8, 128), 1)
    at = iota((256, 128), 1)
    if pack:
        j4, l4 = iota((128 * STEP, 128), 0), iota((128 * STEP, 128), 1)
        slot, j4 = 8 * (i * STEP + (j4 >> 7)), j4 & 127
        left = jnp.where((j4 < 8) & (l4 == slot + j4), 1.0, 0.0).astype(BF16)
        right = jnp.where((j4 >= 120) & (l4 == slot + j4 - 104), 1.0, 0.0).astype(BF16)
        for c in range(2):
            for ref, src, sel in ((packs[0], data[0], left), (packs[1], data[3], right)):
                side = jnp.concatenate([src[e, c] for e in range(STEP)], axis=1)
                ref[c] += dot(side, sel).astype(BF16)
    for e in range(STEP):
        d = i * STEP + e
        for n, t in enumerate(tiles):
            row_shift = off_ref[t, 0, d]
            k = (off_ref[t, 1, d] + 3 - lane) & 127
            base = jnp.zeros((8, 128), F32)
            for tap in range(TAPS):
                base = jnp.where(k == tap, taps_ref[d, tap], base)
            ring = pltpu.roll(jnp.concatenate([base] * 16, axis=0), 0, 1, stride=1, stride_axis=0)
            rows = []
            for part in split(ring):
                own = part * near
                far = part - own
                if t in (0, 3):
                    far = far.astype(F32)
                    edge = jnp.concatenate([far[120:128] if t == 0 else far[0:8]] * 16, axis=0)
                    keep = j < 16 if t == 0 else j >= 112
                    slot = 2 + d if t == 0 else d
                    far = jnp.where(keep, far, jnp.where((j >> 3) == slot, edge, 0.0)).astype(BF16)
                rows.append(jnp.concatenate([own, far], axis=0))
            weights = jnp.concatenate(rows, axis=1)
            parts = []
            for c in range(2):
                cur = data[t][e, c]
                if t == 0:
                    mixed = jnp.where(at < 16, data[1][e, c], halo[0][c])
                elif t == 3:
                    mixed = jnp.where(at < 112, halo[3][c], data[2][e, c])
                else:
                    mixed = jnp.where(at < 64, data[t + 1][e, c], data[t - 1][e, c])
                lhs = jnp.concatenate([cur, mixed], axis=1)
                wide = dot(lhs, weights)
                parts.append((wide[:, :128] + wide[:, 128:]).astype(BF16))
            both = jnp.concatenate(parts, axis=1)
            order = [
                perm[row_shift + 2, pl.ds(pl.multiple_of(64 * ((x_ref[0] + g) & 3), 64), 64), :]
                for g in range(4)
            ]
            moved = dot(jnp.concatenate(order, axis=0), both).astype(BF16)
            for g in range(4):
                for c in range(2):
                    outs[g][n, e, c] = moved[64 * g : 64 * g + 64, 128 * c : 128 * c + 128]


def resample(tiles, slc, halos, offs, taps, x, pack):
    needed = {s for t in tiles for s in (t - 1, t, t + 1) if 0 <= s < 4}
    needed = sorted(needed | {0, 3} if pack else needed)
    halo_in = [t for t in tiles if t in (0, 3)]
    count = len(tiles)
    whole = pl.BlockSpec((2, 256, 128), lambda d, *_: (0, 0, 0))
    in_specs = [
        pl.BlockSpec((STEP, 2, 256, 128), functools.partial(lambda t, d, *_: (d, 0, 0, t), t))
        for t in needed
    ] + [pl.BlockSpec(memory_space=pltpu.VMEM)] * len(halo_in)
    in_specs.append(pl.BlockSpec((5, 256, 256), lambda d, *_: (0, 0, 0)))
    out_specs = [pl.BlockSpec((count, STEP, 2, 64, 128), lambda d, *_: (0, d, 0, 0, 0))] * 4
    out_shape = [jax.ShapeDtypeStruct((count, UNIT, 2, 64, 128), BF16)] * 4
    if pack:
        out_specs += [whole] * 2
        out_shape += [jax.ShapeDtypeStruct((2, 256, 128), BF16)] * 2
    return pl.pallas_call(
        functools.partial(resample_kernel, tiles, needed, halo_in, pack),
        out_shape=out_shape,
        grid_spec=pltpu.PrefetchScalarGridSpec(
            num_scalar_prefetch=3,
            grid=(UNIT // STEP,),
            in_specs=in_specs,
            out_specs=out_specs,
        ),
    )(offs, taps, x, *([slc] * len(needed)), *[halos[t] for t in halo_in], jnp.asarray(row_moves(), BF16))


def table_kernel(first_ref, pairs_ref, out_ref):
    a, b = pairs_ref[0:1, :], pairs_ref[1:2, :]
    date = (iota((REFS, PAIRS), 0) + first_ref[0]) & (DATES - 1)
    key = jnp.where(a == date, iota((REFS, PAIRS), 1) * DATES + b, 1 << 20)
    lane = iota((REFS, 128), 1)
    w = iota((REFS, 128), 0)
    out = jnp.zeros((REFS, 128), jnp.int32)
    for s in range(SLOTS):
        low = jnp.min(key, axis=1, keepdims=True)
        key = jnp.where(key == low, 1 << 20, key)
        away = ((low & (DATES - 1)) - w - first_ref[0]) & (DATES - 1)
        out = jnp.where(lane == s, w + away, out)
    out_ref[...] = out


def table(first, pairs_t):
    return pl.pallas_call(
        table_kernel,
        out_shape=jax.ShapeDtypeStruct((REFS, 128), jnp.int32),
        grid_spec=pltpu.PrefetchScalarGridSpec(
            num_scalar_prefetch=1,
            grid=(1,),
            in_specs=[pl.BlockSpec((2, PAIRS), lambda i, *_: (0, 0))],
            out_specs=pl.BlockSpec((REFS, 128), lambda i, *_: (0, 0)),
        ),
        name="table",
    )(first, pairs_t)


def inverse_kernel(pairs_ref, out_ref):
    date = iota((DATES, PAIRS), 0)
    one = jnp.where(pairs_ref[0:1, :] == date, 1.0, 0.0)
    design = (one - jnp.where(pairs_ref[1:2, :] == date, 1.0, 0.0)).astype(BF16)
    graph = lax.dot_general(
        design, design, (((1,), (1,)), ((), ())), preferred_element_type=F32
    )
    eye = jnp.where(iota((DATES, DATES), 0) == iota((DATES, DATES), 1), 1.0, 0.0)
    top = 2.0 * jnp.max(graph, keepdims=True) + REG
    rho = (top - REG) / (top + REG)
    start = 2.0 / (top + REG)
    square = rho * rho
    beta = 2.0 / (2.0 - square)
    rho = square / (2.0 - square)
    x = (beta * start) * (2.0 * eye - start * (graph + REG * eye))
    whole = graph.astype(BF16)

    def step(_, carry):
        x, rho = carry
        square = rho * rho
        beta = 2.0 / (2.0 - square)
        high, mid = split(x)
        low = (x - high.astype(F32) - mid.astype(F32)).astype(BF16)
        gap = eye - REG * x - (dot(whole, low) + dot(whole, mid) + dot(whole, high))
        gap_h, gap_l = split(gap)
        more = dot(high, gap_l) + dot(mid, gap_h) + dot(high, gap_h)
        return beta * (x + more), square / (2.0 - square)

    out_ref[...] = lax.fori_loop(0, NEWTON, step, (x, rho))[0]


def inverse(pairs_t):
    return pl.pallas_call(
        inverse_kernel,
        out_shape=jax.ShapeDtypeStruct((DATES, DATES), F32),
        name="inverse",
    )(pairs_t)


HALF = 16
RAW = HALF * SLOTS * 8


def fold(v):
    return v[0:16] + v[16:32] + v[32:48] + v[48:64]


def copies_of(sources, win, sem, count):
    return [
        [
            pltpu.make_async_copy(src.at[n], win.at[n, pl.ds(UNIT * u, UNIT)], sem.at[n, u])
            for u, src in sources
        ]
        for n in range(count)
    ]


def look_sums(tiles, copies, tab_ref, place, dates, win, sums, squares, raw, power, before):
    for group in copies:
        for copy in group:
            copy.start()
    k, l = iota((512, 128), 0), iota((512, 128), 1)
    kp, lp = iota((256, 128), 0), iota((256, 128), 1)
    for n, t in enumerate(tiles):
        sel = jnp.where(l == 32 * (k >> 7) + 8 * t + ((k & 127) >> 4), 1.0, 0.0).astype(BF16)
        selp = jnp.where(
            (lp & 63) == 32 * (kp >> 7) + 8 * t + ((kp & 127) >> 4), 1.0, 0.0
        ).astype(BF16)
        for copy in copies[n]:
            copy.wait()
        row = 0
        for start, stop in dates:

            def power_step(i, _):
                tops = []
                for e in range(4):
                    v = win[n, start + 4 * i + e].astype(F32)
                    tops.append(fold(v[0] * v[0] + v[1] * v[1]))
                at = pl.ds(pl.multiple_of(row + i * 32, 32), 32)
                for h in range(2):
                    v = jnp.concatenate([v[8 * h : 8 * h + 8] for v in tops], axis=0)
                    for m, half in enumerate(split(v)):
                        squares[m, at, 128 * h : 128 * h + 128] = half
                return 0

            lax.fori_loop(0, (stop - start) // 4, power_step, 0, unroll=2)
            row += 8 * (stop - start)
        total = dot(squares[0], selp) + dot(squares[1], selp)
        if n > 0:
            total = total + power[...]
        elif before:
            total = total + before[1][...]
        power[...] = total

        def pair_step(i, _):
            w = place(i)
            a = win[n, w].astype(F32)
            for half in range(2):
                got = []
                for s in (2 * half, 2 * half + 1):
                    b = win[n, tab_ref[w, s]].astype(F32)
                    re = fold(a[0] * b[0] + a[1] * b[1])
                    im = fold(a[1] * b[0] - a[0] * b[1])
                    got.append((re[0:8], re[8:16], im[0:8], im[8:16]))
                at = pl.ds(pl.multiple_of(i * 32 + 16 * half, 16), 16)
                for g in range(4):
                    v = jnp.concatenate([got[0][g], got[1][g]], axis=0)
                    for m, part in enumerate(split(v)):
                        sums[m, at, 128 * g : 128 * g + 128] = part
            return 0

        lax.fori_loop(0, HALF, pair_step, 0, unroll=UNROLL)
        looks = dot(sums[0], sel) + dot(sums[1], sel)
        if n > 0:
            looks = looks + raw[...]
        elif before:
            looks = looks + before[0][...]
        raw[...] = looks


def scale_and_scatter(tab_ref, place, raw, whole, rhs):
    for s in range(SLOTS):
        rhs[s] = jnp.zeros_like(rhs[s])

    def scale_step(i, _):
        w = place(i)
        pa = whole[pl.ds(pl.multiple_of(w * 8, 8), 8), :]
        total = jnp.zeros((8, 128), F32)
        for s in range(SLOTS):
            pb = whole[pl.ds(pl.multiple_of(tab_ref[w, s] * 8, 8), 8), :]
            at = pl.multiple_of(i * 32 + 8 * s, 8)
            v = raw[pl.ds(at, 8), :] * lax.rsqrt(pa * pb + EPS)
            total = total + v
            raw[pl.ds(at, 8), :] = v
        rhs[SLOTS, pl.ds(pl.multiple_of(w * 8, 8), 8), :] += total
        return 0

    lax.fori_loop(0, HALF, scale_step, 0, unroll=4)

    def scatter_step(i, _):
        for s in range(SLOTS):
            at = pl.multiple_of(tab_ref[place(i), s] * 8, 8)
            rhs[s, pl.ds(at, 8), :] -= raw[pl.ds(pl.multiple_of(i * 32 + 8 * s, 8), 8), :]
        return 0

    lax.fori_loop(0, HALF, scatter_step, 0, unroll=4)
    rhs[SLOTS] = (rhs[0] + rhs[1]) + (rhs[2] + rhs[3]) + rhs[SLOTS]


def inner_kernel(tiles, first, last, tab_ref, *refs):
    refs = list(refs)
    mine = [refs.pop(0) for _ in range(4)]
    before = () if first else (refs.pop(0), refs.pop(0))
    if last:
        rhs_out, power, win, sums, squares, sem, raw, whole, rhs = refs
    else:
        raw, power, win, sums, squares, sem = refs
    copies = copies_of([(u + 1, mine[u]) for u in range(4)], win, sem, len(tiles))

    def place(i):
        return i + INNER[0]

    look_sums(
        tiles, copies, tab_ref, place, ((8, 40),), win, sums, squares, raw, power, before
    )
    if last:
        whole[64:320] = power[...]
        rhs[SLOTS] = jnp.zeros_like(rhs[SLOTS])
        scale_and_scatter(tab_ref, place, raw, whole, rhs)
        rhs_out[...] = rhs[SLOTS]


def outer_kernel(tiles, first, last, tab_ref, *refs):
    refs = list(refs)
    units = [refs.pop(0) for _ in range(6)]
    before = () if first else (refs.pop(0), refs.pop(0))
    if last:
        inner_rhs, inner_power = refs.pop(0), refs.pop(0)
        out_ref, win, sums, squares, sem, raw, power, whole, rhs = refs
    else:
        raw, power, win, sums, squares, sem = refs
    copies = copies_of(list(enumerate(units)), win, sem, len(tiles))

    def place(i):
        return jnp.where(i < INNER[0], i, i + INNER[1] - INNER[0])

    look_sums(
        tiles,
        copies,
        tab_ref,
        place,
        ((0, 8), (40, 48)),
        win,
        sums,
        squares,
        raw,
        power,
        before,
    )
    if last:
        whole[0:64] = power[0:64]
        whole[64:320] = inner_power[...]
        whole[320:384] = power[64:128]
        rhs[SLOTS] = inner_rhs[...]
        scale_and_scatter(tab_ref, place, raw, whole, rhs)
        for z in range(8):
            out_ref[z] = rhs[SLOTS, pl.ds(z, WINDOW, stride=8), :]


def coherence(inner, tiles, tab, units, before, extra, last):
    count = len(tiles)
    rows = 256 if inner else 128
    vmem = pl.BlockSpec(memory_space=pltpu.VMEM)
    raw = jax.ShapeDtypeStruct((RAW, 128), F32)
    power = jax.ShapeDtypeStruct((rows, 128), F32)
    scratch = [
        pltpu.VMEM((count, WINDOW, 2, 64, 128), BF16),
        pltpu.VMEM((2, RAW, 512), BF16),
        pltpu.VMEM((2, rows, 256), BF16),
        pltpu.SemaphoreType.DMA((count, 6)),
    ]
    outs = [raw, power]
    if last:
        scratch.append(pltpu.VMEM((RAW, 128), F32))
        if inner:
            outs = [jax.ShapeDtypeStruct((WINDOW * 8, 128), F32), power]
        else:
            outs = jax.ShapeDtypeStruct((8, WINDOW, 128), F32)
            scratch.append(pltpu.VMEM((rows, 128), F32))
        scratch += [
            pltpu.VMEM((WINDOW * 8, 128), F32),
            pltpu.VMEM((SLOTS + 1, WINDOW * 8, 128), F32),
        ]
    return pl.pallas_call(
        functools.partial(inner_kernel if inner else outer_kernel, tiles, not before, last),
        out_shape=outs,
        in_specs=[pl.BlockSpec(memory_space=pltpu.SMEM)]
        + [vmem if not inner and u in (0, 5) else pl.BlockSpec(memory_space=pl.ANY) for u in range(len(units))]
        + [vmem] * len((*before, *extra)),
        out_specs=[vmem] * 2 if isinstance(outs, list) else vmem,
        scratch_shapes=scratch,
    )(tab, *units, *before, *extra)


def solve_kernel(inv_ref, got_ref, out_ref, rhs):
    for z in range(8):
        early = got_ref[z, 0:16, :] + got_ref[(z + 7) % 8, 32:48, :]
        rhs[32 * z : 32 * z + 16, :] = early
        rhs[32 * z + 16 : 32 * z + 32, :] = got_ref[z, 16:32, :]
        if z == 0:
            rhs[DATES : DATES + 8, :] = early[0:8]
    out_ref[...] = lax.dot_general(
        rhs[8 : DATES + 8, :],
        inv_ref[...],
        (((0,), (0,)), ((), ())),
        precision=lax.Precision.HIGHEST,
        preferred_element_type=F32,
    )


def solve(inv, got):
    return pl.pallas_call(
        solve_kernel,
        out_shape=jax.ShapeDtypeStruct((128, DATES), F32),
        in_specs=[pl.BlockSpec(memory_space=pltpu.VMEM)] * 2,
        out_specs=pl.BlockSpec(memory_space=pltpu.VMEM),
        scratch_shapes=[pltpu.VMEM((DATES + 8, 128), F32)],
        name="solve",
    )(inv, got)


def arrange_kernel(x_ref, *refs):
    sources, outs = refs[:4], refs[4:]
    for u in range(4):
        for away in range(4):

            @pl.when(((u - x_ref[0]) & 3) == away)
            def _():
                outs[u][...] = sources[away][...]


def arrange(x, pieces):
    vmem = pl.BlockSpec(memory_space=pltpu.VMEM)
    return pl.pallas_call(
        arrange_kernel,
        out_shape=[jax.ShapeDtypeStruct(p.shape, p.dtype) for p in pieces],
        in_specs=[pl.BlockSpec(memory_space=pltpu.SMEM)] + [vmem] * 4,
        out_specs=[vmem] * 4,
    )(x, *pieces)


def near_by(v):
    return pltpu.with_memory_space_constraint(v, pltpu.VMEM)


def shift(v, axis, step):
    size = lax.axis_size(axis)
    return lax.ppermute(v, axis, [(i, (i + step) % size) for i in range(size)])


def per_device(slc, offsets, taps, pairs):
    x = lax.axis_index("x").astype(jnp.int32)
    first = lax.axis_index("z").astype(jnp.int32) * 32 - 8
    xs = x.reshape(1)
    pairs_t = pairs.T
    offs = jnp.transpose(offsets, (1, 2, 0))
    halos = {}
    units = []
    for n, tiles in enumerate(CHUNKS):
        got = resample(tiles, slc, halos, offs, taps, xs, n == 0)
        if n == 0:
            size = lax.axis_size("rng")
            halos[3] = near_by(lax.ppermute(got[4], "rng", [(i + 1, i) for i in range(size - 1)]))
            halos[0] = near_by(lax.ppermute(got[5], "rng", [(i, i + 1) for i in range(size - 1)]))
        own, ahead, across, behind = got[:4]
        plus2 = near_by(shift(across, "x", 2))
        minus1 = near_by(shift(ahead, "x", 1))
        plus1 = near_by(shift(behind, "x", -1))
        mine = arrange(xs, (own, plus1, plus2, minus1))
        below = near_by(shift(mine[3], "z", 1))
        above = near_by(shift(mine[0], "z", -1))
        units.append((below, *mine, above))
    tab = table(first.reshape(1), pairs_t)
    inv = inverse(pairs_t)
    ins, outs = (), ()
    for n, tiles in enumerate(CHUNKS):
        last = n == len(CHUNKS) - 1
        ins = coherence(True, tiles, tab, units[n][1:5], ins, (), last)
        outs = coherence(False, tiles, tab, units[n], outs, ins if last else (), last)
    got = near_by(lax.all_to_all(outs, "z", split_axis=0, concat_axis=0, tiled=True))
    series = solve(inv, got)
    return jnp.transpose(series.reshape(2, 2, 32, DATES), (0, 3, 1, 2))


def solution(mesh):
    fine = Mesh(mesh.devices.reshape(8, 4, 8), ("z", "x", "rng"))
    date = ("z", "x")
    return jax.shard_map(
        per_device,
        mesh=fine,
        in_specs=(P(date, None, None, "rng"), P(date, "rng", None), P(date, None), P()),
        out_specs=P(None, None, date, "rng"),
        check_vma=False,
    )
```

```python
import functools

import jax
import jax.numpy as jnp
import numpy as np
from jax import lax
from jax.experimental import pallas as pl
from jax.experimental.pallas import tpu as pltpu
from jax.sharding import Mesh
from jax.sharding import PartitionSpec as P


TAPS = 8
EPS = 1e-06
REG = 0.1
DATES = 256
PAIRS = 1024
UNIT = 8
WINDOW = 48
REFS = 32
INNER = (8, 24)
SLOTS = 4
NEWTON = 9
UNROLL = 4
STEP = 4
CHUNKS = ((1, 2), (0, 3))

F32 = jnp.float32
BF16 = jnp.bfloat16


def iota(shape, dim):
    return lax.broadcasted_iota(jnp.int32, shape, dim)


def dot(a, b, precision=None):
    return jnp.dot(a, b, precision=precision, preferred_element_type=F32)


def split(v):
    high = v.astype(BF16)
    return high, (v - high.astype(F32)).astype(BF16)


def row_moves():
    o = np.arange(256)[:, None]
    row = 32 * (o & 7) + 8 * (o >> 6) + 4 * ((o >> 3) & 1) + ((o >> 4) & 3)
    shift = np.arange(-2, 3)[:, None, None]
    return (row - shift == np.arange(256)).astype(np.float32)


def resample_kernel(tiles, needed, halo_in, pack, off_ref, taps_ref, x_ref, *refs):
    refs = list(refs)
    data = {t: refs.pop(0) for t in needed}
    halo = {t: refs.pop(0) for t in halo_in}
    perm = refs.pop(0)
    outs = [refs.pop(0) for _ in range(4)]
    packs = [refs.pop(0) for _ in range(2)] if pack else None
    i = pl.program_id(0)
    if pack:

        @pl.when(i == 0)
        def _():
            for ref in packs:
                ref[...] = jnp.zeros_like(ref)

    j, l = iota((128, 128), 0), iota((128, 128), 1)
    near = jnp.where(jnp.abs(j - l) < 64, 1.0, 0.0).astype(BF16)
    lane = iota((8, 128), 1)
    at = iota((256, 128), 1)
    if pack:
        j4, l4 = iota((128 * STEP, 128), 0), iota((128 * STEP, 128), 1)
        slot, j4 = 8 * (i * STEP + (j4 >> 7)), j4 & 127
        left = jnp.where((j4 < 8) & (l4 == slot + j4), 1.0, 0.0).astype(BF16)
        right = jnp.where((j4 >= 120) & (l4 == slot + j4 - 104), 1.0, 0.0).astype(BF16)
        for c in range(2):
            for ref, src, sel in ((packs[0], data[0], left), (packs[1], data[3], right)):
                side = jnp.concatenate([src[e, c] for e in range(STEP)], axis=1)
                ref[c] += dot(side, sel).astype(BF16)
    for e in range(STEP):
        d = i * STEP + e
        for n, t in enumerate(tiles):
            row_shift = off_ref[t, 0, d]
            k = (off_ref[t, 1, d] + 3 - lane) & 127
            base = jnp.zeros((8, 128), F32)
            for tap in range(TAPS):
                base = jnp.where(k == tap, taps_ref[d, tap], base)
            ring = pltpu.roll(jnp.concatenate([base] * 16, axis=0), 0, 1, stride=1, stride_axis=0)
            rows = []
            for part in split(ring):
                own = part * near
                far = part - own
                if t in (0, 3):
                    far = far.astype(F32)
                    edge = jnp.concatenate([far[120:128] if t == 0 else far[0:8]] * 16, axis=0)
                    keep = j < 16 if t == 0 else j >= 112
                    slot = 2 + d if t == 0 else d
                    far = jnp.where(keep, far, jnp.where((j >> 3) == slot, edge, 0.0)).astype(BF16)
                rows.append(jnp.concatenate([own, far], axis=0))
            weights = jnp.concatenate(rows, axis=1)
            parts = []
            for c in range(2):
                cur = data[t][e, c]
                if t == 0:
                    mixed = jnp.where(at < 16, data[1][e, c], halo[0][c])
                elif t == 3:
                    mixed = jnp.where(at < 112, halo[3][c], data[2][e, c])
                else:
                    mixed = jnp.where(at < 64, data[t + 1][e, c], data[t - 1][e, c])
                lhs = jnp.concatenate([cur, mixed], axis=1)
                wide = dot(lhs, weights)
                parts.append((wide[:, :128] + wide[:, 128:]).astype(BF16))
            both = jnp.concatenate(parts, axis=1)
            order = [
                perm[row_shift + 2, pl.ds(pl.multiple_of(64 * ((x_ref[0] + g) & 3), 64), 64), :]
                for g in range(4)
            ]
            moved = dot(jnp.concatenate(order, axis=0), both).astype(BF16)
            for g in range(4):
                for c in range(2):
                    outs[g][n, e, c] = moved[64 * g : 64 * g + 64, 128 * c : 128 * c + 128]


def resample(tiles, slc, halos, offs, taps, x, pack):
    needed = {s for t in tiles for s in (t - 1, t, t + 1) if 0 <= s < 4}
    needed = sorted(needed | {0, 3} if pack else needed)
    halo_in = [t for t in tiles if t in (0, 3)]
    count = len(tiles)
    whole = pl.BlockSpec((2, 256, 128), lambda d, *_: (0, 0, 0))
    in_specs = [
        pl.BlockSpec((STEP, 2, 256, 128), functools.partial(lambda t, d, *_: (d, 0, 0, t), t))
        for t in needed
    ] + [pl.BlockSpec(memory_space=pltpu.VMEM)] * len(halo_in)
    in_specs.append(pl.BlockSpec((5, 256, 256), lambda d, *_: (0, 0, 0)))
    out_specs = [pl.BlockSpec((count, STEP, 2, 64, 128), lambda d, *_: (0, d, 0, 0, 0))] * 4
    out_shape = [jax.ShapeDtypeStruct((count, UNIT, 2, 64, 128), BF16)] * 4
    if pack:
        out_specs += [whole] * 2
        out_shape += [jax.ShapeDtypeStruct((2, 256, 128), BF16)] * 2
    return pl.pallas_call(
        functools.partial(resample_kernel, tiles, needed, halo_in, pack),
        out_shape=out_shape,
        grid_spec=pltpu.PrefetchScalarGridSpec(
            num_scalar_prefetch=3,
            grid=(UNIT // STEP,),
            in_specs=in_specs,
            out_specs=out_specs,
        ),
    )(offs, taps, x, *([slc] * len(needed)), *[halos[t] for t in halo_in], jnp.asarray(row_moves(), BF16))


def table_kernel(first_ref, pairs_ref, out_ref):
    a, b = pairs_ref[0:1, :], pairs_ref[1:2, :]
    date = (iota((REFS, PAIRS), 0) + first_ref[0]) & (DATES - 1)
    key = jnp.where(a == date, iota((REFS, PAIRS), 1) * DATES + b, 1 << 20)
    lane = iota((REFS, 128), 1)
    w = iota((REFS, 128), 0)
    out = jnp.zeros((REFS, 128), jnp.int32)
    for s in range(SLOTS):
        low = jnp.min(key, axis=1, keepdims=True)
        key = jnp.where(key == low, 1 << 20, key)
        away = ((low & (DATES - 1)) - w - first_ref[0]) & (DATES - 1)
        out = jnp.where(lane == s, w + away, out)
    out_ref[...] = out


def table(first, pairs_t):
    return pl.pallas_call(
        table_kernel,
        out_shape=jax.ShapeDtypeStruct((REFS, 128), jnp.int32),
        grid_spec=pltpu.PrefetchScalarGridSpec(
            num_scalar_prefetch=1,
            grid=(1,),
            in_specs=[pl.BlockSpec((2, PAIRS), lambda i, *_: (0, 0))],
            out_specs=pl.BlockSpec((REFS, 128), lambda i, *_: (0, 0)),
        ),
        name="table",
    )(first, pairs_t)


def inverse_kernel(pairs_ref, out_ref):
    date = iota((DATES, PAIRS), 0)
    one = jnp.where(pairs_ref[0:1, :] == date, 1.0, 0.0)
    design = (one - jnp.where(pairs_ref[1:2, :] == date, 1.0, 0.0)).astype(BF16)
    graph = lax.dot_general(
        design, design, (((1,), (1,)), ((), ())), preferred_element_type=F32
    )
    eye = jnp.where(iota((DATES, DATES), 0) == iota((DATES, DATES), 1), 1.0, 0.0)
    top = 2.0 * jnp.max(graph, keepdims=True) + REG
    rho = (top - REG) / (top + REG)
    start = 2.0 / (top + REG)
    square = rho * rho
    beta = 2.0 / (2.0 - square)
    rho = square / (2.0 - square)
    x = (beta * start) * (2.0 * eye - start * (graph + REG * eye))
    whole = graph.astype(BF16)

    def step(_, carry):
        x, rho = carry
        square = rho * rho
        beta = 2.0 / (2.0 - square)
        high, mid = split(x)
        low = (x - high.astype(F32) - mid.astype(F32)).astype(BF16)
        gap = eye - REG * x - (dot(whole, low) + dot(whole, mid) + dot(whole, high))
        gap_h, gap_l = split(gap)
        more = dot(high, gap_l) + dot(mid, gap_h) + dot(high, gap_h)
        return beta * (x + more), square / (2.0 - square)

    out_ref[...] = lax.fori_loop(0, NEWTON, step, (x, rho))[0]


def inverse(pairs_t):
    return pl.pallas_call(
        inverse_kernel,
        out_shape=jax.ShapeDtypeStruct((DATES, DATES), F32),
        name="inverse",
    )(pairs_t)


HALF = 16
RAW = HALF * SLOTS * 8


def fold(v):
    return v[0:16] + v[16:32] + v[32:48] + v[48:64]


def copies_of(sources, win, sem, count):
    return [
        [
            pltpu.make_async_copy(src.at[n], win.at[n, pl.ds(UNIT * u, UNIT)], sem.at[n, u])
            for u, src in sources
        ]
        for n in range(count)
    ]


def look_sums(tiles, copies, tab_ref, place, dates, win, sums, squares, raw, power, before):
    for group in copies:
        for copy in group:
            copy.start()
    k, l = iota((512, 128), 0), iota((512, 128), 1)
    kp, lp = iota((256, 128), 0), iota((256, 128), 1)
    for n, t in enumerate(tiles):
        sel = jnp.where(l == 32 * (k >> 7) + 8 * t + ((k & 127) >> 4), 1.0, 0.0).astype(BF16)
        selp = jnp.where(
            (lp & 63) == 32 * (kp >> 7) + 8 * t + ((kp & 127) >> 4), 1.0, 0.0
        ).astype(BF16)
        for copy in copies[n]:
            copy.wait()
        row = 0
        for start, stop in dates:

            def power_step(i, _):
                tops = []
                for e in range(4):
                    v = win[n, start + 4 * i + e].astype(F32)
                    tops.append(fold(v[0] * v[0] + v[1] * v[1]))
                at = pl.ds(pl.multiple_of(row + i * 32, 32), 32)
                for h in range(2):
                    v = jnp.concatenate([v[8 * h : 8 * h + 8] for v in tops], axis=0)
                    for m, half in enumerate(split(v)):
                        squares[m, at, 128 * h : 128 * h + 128] = half
                return 0

            lax.fori_loop(0, (stop - start) // 4, power_step, 0, unroll=2)
            row += 8 * (stop - start)
        total = dot(squares[0], selp) + dot(squares[1], selp)
        if n > 0:
            total = total + power[...]
        elif before:
            total = total + before[1][...]
        power[...] = total

        def pair_step(i, _):
            w = place(i)
            a = win[n, w].astype(F32)
            for half in range(2):
                got = []
                for s in (2 * half, 2 * half + 1):
                    b = win[n, tab_ref[w, s]].astype(F32)
                    re = fold(a[0] * b[0] + a[1] * b[1])
                    im = fold(a[1] * b[0] - a[0] * b[1])
                    got.append((re[0:8], re[8:16], im[0:8], im[8:16]))
                at = pl.ds(pl.multiple_of(i * 32 + 16 * half, 16), 16)
                for g in range(4):
                    v = jnp.concatenate([got[0][g], got[1][g]], axis=0)
                    for m, part in enumerate(split(v)):
                        sums[m, at, 128 * g : 128 * g + 128] = part
            return 0

        lax.fori_loop(0, HALF, pair_step, 0, unroll=UNROLL)
        looks = dot(sums[0], sel) + dot(sums[1], sel)
        if n > 0:
            looks = looks + raw[...]
        elif before:
            looks = looks + before[0][...]
        raw[...] = looks


def scale_and_scatter(tab_ref, place, raw, whole, rhs):
    for s in range(SLOTS):
        rhs[s] = jnp.zeros_like(rhs[s])

    def scale_step(i, _):
        w = place(i)
        pa = whole[pl.ds(pl.multiple_of(w * 8, 8), 8), :]
        total = jnp.zeros((8, 128), F32)
        for s in range(SLOTS):
            pb = whole[pl.ds(pl.multiple_of(tab_ref[w, s] * 8, 8), 8), :]
            at = pl.multiple_of(i * 32 + 8 * s, 8)
            v = raw[pl.ds(at, 8), :] * lax.rsqrt(pa * pb + EPS)
            total = total + v
            raw[pl.ds(at, 8), :] = v
        rhs[SLOTS, pl.ds(pl.multiple_of(w * 8, 8), 8), :] += total
        return 0

    lax.fori_loop(0, HALF, scale_step, 0, unroll=4)

    def scatter_step(i, _):
        for s in range(SLOTS):
            at = pl.multiple_of(tab_ref[place(i), s] * 8, 8)
            rhs[s, pl.ds(at, 8), :] -= raw[pl.ds(pl.multiple_of(i * 32 + 8 * s, 8), 8), :]
        return 0

    lax.fori_loop(0, HALF, scatter_step, 0, unroll=4)
    rhs[SLOTS] = (rhs[0] + rhs[1]) + (rhs[2] + rhs[3]) + rhs[SLOTS]


def inner_kernel(tiles, first, last, tab_ref, *refs):
    refs = list(refs)
    mine = [refs.pop(0) for _ in range(4)]
    before = () if first else (refs.pop(0), refs.pop(0))
    if last:
        rhs_out, power, win, sums, squares, sem, raw, whole, rhs = refs
    else:
        raw, power, win, sums, squares, sem = refs
    copies = copies_of([(u + 1, mine[u]) for u in range(4)], win, sem, len(tiles))

    def place(i):
        return i + INNER[0]

    look_sums(
        tiles, copies, tab_ref, place, ((8, 40),), win, sums, squares, raw, power, before
    )
    if last:
        whole[64:320] = power[...]
        rhs[SLOTS] = jnp.zeros_like(rhs[SLOTS])
        scale_and_scatter(tab_ref, place, raw, whole, rhs)
        rhs_out[...] = rhs[SLOTS]


def outer_kernel(tiles, first, last, tab_ref, *refs):
    refs = list(refs)
    units = [refs.pop(0) for _ in range(6)]
    before = () if first else (refs.pop(0), refs.pop(0))
    if last:
        inner_rhs, inner_power = refs.pop(0), refs.pop(0)
        out_ref, win, sums, squares, sem, raw, power, whole, rhs = refs
    else:
        raw, power, win, sums, squares, sem = refs
    copies = copies_of(list(enumerate(units)), win, sem, len(tiles))

    def place(i):
        return jnp.where(i < INNER[0], i, i + INNER[1] - INNER[0])

    look_sums(
        tiles,
        copies,
        tab_ref,
        place,
        ((0, 8), (40, 48)),
        win,
        sums,
        squares,
        raw,
        power,
        before,
    )
    if last:
        whole[0:64] = power[0:64]
        whole[64:320] = inner_power[...]
        whole[320:384] = power[64:128]
        rhs[SLOTS] = inner_rhs[...]
        scale_and_scatter(tab_ref, place, raw, whole, rhs)
        for z in range(8):
            out_ref[z] = rhs[SLOTS, pl.ds(z, WINDOW, stride=8), :]


def coherence(inner, tiles, tab, units, before, extra, last):
    count = len(tiles)
    rows = 256 if inner else 128
    vmem = pl.BlockSpec(memory_space=pltpu.VMEM)
    raw = jax.ShapeDtypeStruct((RAW, 128), F32)
    power = jax.ShapeDtypeStruct((rows, 128), F32)
    scratch = [
        pltpu.VMEM((count, WINDOW, 2, 64, 128), BF16),
        pltpu.VMEM((2, RAW, 512), BF16),
        pltpu.VMEM((2, rows, 256), BF16),
        pltpu.SemaphoreType.DMA((count, 6)),
    ]
    outs = [raw, power]
    if last:
        scratch.append(pltpu.VMEM((RAW, 128), F32))
        if inner:
            outs = [jax.ShapeDtypeStruct((WINDOW * 8, 128), F32), power]
        else:
            outs = jax.ShapeDtypeStruct((8, WINDOW, 128), F32)
            scratch.append(pltpu.VMEM((rows, 128), F32))
        scratch += [
            pltpu.VMEM((WINDOW * 8, 128), F32),
            pltpu.VMEM((SLOTS + 1, WINDOW * 8, 128), F32),
        ]
    return pl.pallas_call(
        functools.partial(inner_kernel if inner else outer_kernel, tiles, not before, last),
        out_shape=outs,
        in_specs=[pl.BlockSpec(memory_space=pltpu.SMEM)]
        + [vmem] * len(units)
        + [vmem] * len((*before, *extra)),
        out_specs=[vmem] * 2 if isinstance(outs, list) else vmem,
        scratch_shapes=scratch,
        compiler_params=pltpu.CompilerParams(vmem_limit_bytes=24 << 20),
    )(tab, *units, *before, *extra)


def solve_kernel(inv_ref, got_ref, out_ref, rhs):
    for z in range(8):
        early = got_ref[z, 0:16, :] + got_ref[(z + 7) % 8, 32:48, :]
        rhs[32 * z : 32 * z + 16, :] = early
        rhs[32 * z + 16 : 32 * z + 32, :] = got_ref[z, 16:32, :]
        if z == 0:
            rhs[DATES : DATES + 8, :] = early[0:8]
    out_ref[...] = lax.dot_general(
        rhs[8 : DATES + 8, :],
        inv_ref[...],
        (((0,), (0,)), ((), ())),
        precision=lax.Precision.HIGHEST,
        preferred_element_type=F32,
    )


def solve(inv, got):
    return pl.pallas_call(
        solve_kernel,
        out_shape=jax.ShapeDtypeStruct((128, DATES), F32),
        in_specs=[pl.BlockSpec(memory_space=pltpu.VMEM)] * 2,
        out_specs=pl.BlockSpec(memory_space=pltpu.VMEM),
        scratch_shapes=[pltpu.VMEM((DATES + 8, 128), F32)],
        name="solve",
    )(inv, got)


def arrange_kernel(x_ref, *refs):
    sources, outs = refs[:4], refs[4:]
    for u in range(4):
        for away in range(4):

            @pl.when(((u - x_ref[0]) & 3) == away)
            def _():
                outs[u][...] = sources[away][...]


def arrange(x, pieces):
    vmem = pl.BlockSpec(memory_space=pltpu.VMEM)
    return pl.pallas_call(
        arrange_kernel,
        out_shape=[pltpu.VMEM(p.shape, p.dtype) for p in pieces],
        in_specs=[pl.BlockSpec(memory_space=pltpu.SMEM)] + [vmem] * 4,
        out_specs=[vmem] * 4,
        compiler_params=pltpu.CompilerParams(vmem_limit_bytes=8 << 20),
    )(x, *pieces)


def near_by(v):
    return pltpu.with_memory_space_constraint(v, pltpu.VMEM)


def shift(v, axis, step):
    size = lax.axis_size(axis)
    return lax.ppermute(v, axis, [(i, (i + step) % size) for i in range(size)])


def per_device(slc, offsets, taps, pairs):
    x = lax.axis_index("x").astype(jnp.int32)
    first = lax.axis_index("z").astype(jnp.int32) * 32 - 8
    xs = x.reshape(1)
    pairs_t = pairs.T
    offs = jnp.transpose(offsets, (1, 2, 0))
    halos = {}
    units = []
    for n, tiles in enumerate(CHUNKS):
        got = resample(tiles, slc, halos, offs, taps, xs, n == 0)
        if n == 0:
            size = lax.axis_size("rng")
            halos[3] = near_by(lax.ppermute(got[4], "rng", [(i + 1, i) for i in range(size - 1)]))
            halos[0] = near_by(lax.ppermute(got[5], "rng", [(i, i + 1) for i in range(size - 1)]))
        own, ahead, across, behind = got[:4]
        plus2 = near_by(shift(across, "x", 2))
        minus1 = near_by(shift(ahead, "x", 1))
        plus1 = near_by(shift(behind, "x", -1))
        mine = arrange(xs, (own, plus1, plus2, minus1))
        below = near_by(shift(mine[3], "z", 1))
        above = near_by(shift(mine[0], "z", -1))
        units.append((below, *mine, above))
    tab = table(first.reshape(1), pairs_t)
    inv = inverse(pairs_t)
    ins, outs = (), ()
    for n, tiles in enumerate(CHUNKS):
        last = n == len(CHUNKS) - 1
        ins = coherence(True, tiles, tab, units[n][1:5], ins, (), last)
        outs = coherence(False, tiles, tab, units[n], outs, ins if last else (), last)
    got = near_by(lax.all_to_all(outs, "z", split_axis=0, concat_axis=0, tiled=True))
    series = solve(inv, got)
    return jnp.transpose(series.reshape(2, 2, 32, DATES), (0, 3, 1, 2))


def solution(mesh):
    fine = Mesh(mesh.devices.reshape(8, 4, 8), ("z", "x", "rng"))
    date = ("z", "x")
    return jax.shard_map(
        per_device,
        mesh=fine,
        in_specs=(P(date, None, None, "rng"), P(date, "rng", None), P(date, None), P()),
        out_specs=P(None, None, date, "rng"),
        check_vma=False,
    )
```
